32 devices in a mesh: parts: 2 (over y), ctx: 4 (over z), mp: 4 (over x, core).
Axes of the slice: x: 2, y: 2, z: 4, core: 2. Of those that a mesh axis runs over, the one named last changes fastest.
Arguments:
- inputs: bfloat16 [1024, 3, 4096], P(('parts', 'ctx'), None, 'mp'), parts along dimension 0, may hold values from -6 to 6
- short_filter: bfloat16 [3, 3, 4096], P(None, None, 'mp'), may hold values from -3.5 to 3.5
- long_filter: bfloat16 [256, 128], P('mp'), may hold values from -0.5 to 0.5
- skip_gain: float32 [4096], P('mp'), may hold values from -1 to 1
- queries: bfloat16 [1024, 4096], P(('parts', 'ctx'), 'mp'), parts along dimension 0, may hold values from -6 to 6
- key_rows: bfloat16 [1024, 4096], P(('parts', 'ctx'), 'mp'), parts along dimension 0, may hold values from -6 to 6
- out_weight: bfloat16 [4096, 4096], P('mp'), may hold values from -0.25 to 0.25
Outputs:
- block_output: bfloat16 [1024, 4096], P(('parts', 'ctx'), 'mp'), parts along dimension 0
The draws below stay inside these ranges and needn't reach their ends.
There are 2 independent parts, one for each index of `parts`. The reference program is written for one: setup_inputs(seed, part) draws one part's arguments, and reference() takes and returns one part's arrays. A program takes and returns all parts, laid end to end along the dimension named above; an argument that names none is the same for every part. Nothing has to cross between parts.
All inputs are finite; a program needn't handle non-finite values.
Results may differ from the reference program's by a relative error of at most 0.014.
Values may be sent and summed in bfloat16 or wider, within the bound.
A program may use at most 64 MiB of HBM per device.

```python
import jax
import jax.numpy as jnp
from jax import lax

D = 4096
HEAD_DIM = 128
GROUP = 16
SHORT_K = 3
LONG_K = 128
GROUPS = 256
WINDOW = 512


def drawn_values(key, salt):
    return 1.5 * jax.random.truncated_normal(jax.random.fold_in(key, salt), -4.0, 4.0, (WINDOW, D), jnp.float32)


def draw_queries(key, part):
    values_drawn = drawn_values(key, 1)
    return values_drawn.astype(jnp.bfloat16)


def draw_key_rows(key, part):
    values_drawn = drawn_values(key, 2)
    return values_drawn.astype(jnp.bfloat16)


def raised(array, key, source, target, parts, factor):
    def block_of(position):
        return (jnp.arange(array.shape[position]) // (array.shape[position] // parts)).reshape((-1,) + (1,) * (array.ndim - 1 - position))

    first = jax.random.permutation(key, parts)[block_of(target)]
    other_side = (block_of(target) + parts // 2) % parts
    return jnp.where((block_of(source) == first) | (block_of(source) == other_side), factor * array, array)


def steps_of(rng, shape, cuts, smallest, largest):
    level, own = 1.0, jax.random.fold_in(rng, 6)
    for dim, shards_of in cuts:
        steps = jnp.exp(jax.random.uniform(jax.random.fold_in(own, dim), (shards_of,), jnp.float32, smallest / len(cuts), largest / len(cuts)))
        level = level * jnp.repeat(steps, shape[dim] // shards_of).reshape([-1 if axis == dim else 1 for axis in range(len(shape))])
    return level


def centred(own_key, dims, scale, reach, split=(), dtype=jnp.bfloat16):
    array = jax.random.normal(own_key, dims, jnp.float32) * scale
    if len(split) > 0:
        array = steps_of(own_key, dims, split, -0.22, 0.18) * array
    return jnp.clip(array, min=-reach, max=reach).astype(dtype)


def bell_draw_with(key, dims, width, limit, pieces, heavy, kind=jnp.bfloat16):
    values = width * jax.random.normal(key, dims, jnp.float32)
    if pieces:
        values = values * steps_of(key, dims, pieces, -0.22, 0.18)
    return jnp.clip(raised(values, jax.random.fold_in(key, 3), *heavy), -limit, limit).astype(kind)


def setup_inputs(seed: int = 0, part: int = 0) -> dict:
    splits = jax.random.split(jax.random.key(seed), 8)
    part_keys = jax.random.split(jax.random.fold_in(splits[7], part), 8)
    inputs = centred(part_keys[0], (WINDOW, 3, D), 1.0, 6.0, ((0, 4), (2, 4)))
    short_filter = centred(splits[1], (SHORT_K, 3, D), SHORT_K ** -0.5, 3.5, ((2, 4),))
    long_filter = centred(splits[2], (GROUPS, LONG_K), LONG_K ** -0.5, 0.5, ((0, 4),))
    skip_gain = jnp.clip(jax.random.uniform(splits[3], (D,), jnp.float32, -1.0, 1.0) * steps_of(splits[3], (D,), ((0, 4),), -0.4, 0.0), -1.0, 1.0)
    queries = draw_queries(jax.random.fold_in(jax.random.fold_in(splits[7], part), 71), part)
    key_rows = draw_key_rows(jax.random.fold_in(jax.random.fold_in(splits[7], part), 71), part)
    out_weight = bell_draw_with(splits[6], (D, D), (D // 4) ** -0.5, 0.25, ((0, 4),), (0, 1, 4, 2.0))
    return {"inputs": inputs, "short_filter": short_filter, "long_filter": long_filter, "skip_gain": skip_gain, "queries": queries, "key_rows": key_rows, "out_weight": out_weight}


def reference(inputs, short_filter, long_filter, skip_gain, queries, key_rows, out_weight):
    window = inputs.shape[0]
    signal = inputs.astype(jnp.float32)
    features = jnp.zeros(signal.shape, jnp.float32)
    for lag_index in range(SHORT_K):
        delayed = jnp.pad(signal, ((lag_index, 0), (0, 0), (0, 0)))[:window]
        features = features + short_filter[lag_index].astype(jnp.float32)[None] * delayed
    gate_product = (features[:, 1] * features[:, 2]).astype(jnp.bfloat16)
    gate_float = gate_product.astype(jnp.float32)
    filters = jnp.repeat(long_filter.astype(jnp.float32), GROUP, axis=0)
    padded = jnp.pad(gate_float, ((LONG_K - 1, 0), (0, 0)))

    def add_tap(tap_index, filtered):
        column = lax.dynamic_slice_in_dim(filters, tap_index, 1, 1)[:, 0]
        delayed = lax.dynamic_slice_in_dim(padded, LONG_K - 1 - tap_index, window, 0)
        return filtered + column[None] * delayed

    filtered = lax.fori_loop(0, LONG_K, add_tap, jnp.zeros((window, D), jnp.float32))
    values = (features[:, 0] * (filtered + skip_gain[None] * gate_float)).astype(jnp.bfloat16)
    head_count = D // HEAD_DIM
    head_queries = queries.reshape(window, head_count, HEAD_DIM).transpose(1, 0, 2)
    head_keys = key_rows.reshape(window, head_count, HEAD_DIM).transpose(1, 0, 2)
    head_values = values.reshape(window, head_count, HEAD_DIM).transpose(1, 0, 2)
    causal = jnp.tril(jnp.ones((window, window), jnp.bool_))

    def one_head(operands):
        head_query, head_key, head_value = operands
        scores = jnp.dot(head_query, head_key.T, preferred_element_type=jnp.float32) * (HEAD_DIM ** -0.5)
        new_max = jnp.max(jnp.where(causal, scores, -1e30), axis=1)
        probabilities = jnp.where(causal, jnp.exp(scores - new_max[:, None]), 0.0)
        weight_sum = jnp.sum(probabilities, axis=1)
        mixed = jnp.dot(probabilities.astype(jnp.bfloat16), head_value, preferred_element_type=jnp.float32)
        return (mixed / weight_sum[:, None]).astype(jnp.bfloat16)

    attended = lax.map(one_head, (head_queries, head_keys, head_values))
    attended = attended.transpose(1, 0, 2).reshape(window, D)
    return jnp.dot(attended, out_weight, preferred_element_type=jnp.float32).astype(jnp.bfloat16)
```

```python
import functools

import jax
import jax.numpy as jnp
from jax import lax
from jax.experimental import pallas as pl
from jax.experimental.pallas import tpu as pltpu
from jax.sharding import PartitionSpec as P

HD = 128
MESH = pl.DeviceIdType.MESH
NEG = -1e30
F32 = jnp.float32
BF = jnp.bfloat16


def dot(a, b, ca=1, cb=0):
    return lax.dot_general(a, b, (((ca,), (cb,)), ((), ())), preferred_element_type=F32)


def kernel(
    n, m, x_hbm, sf_hbm, lf_hbm, skip_hbm, q_hbm, k_hbm, w_hbm, out_ref,
    sf_ref, lf_ref, skip_ref, psem, xb, rim_out, rim_in, f0, gown, gprev, taps, kbuf, vbuf, qbuf, mst, lst, ast,
    sbuf, sstat, pbuf, pstat, att, wv, acc, s1, r1, s2, r2,
    xsem, qsem, ksem, wsem, rim_s, rim_r, gate_s, gate_r, k_s, k_r, v_s, v_r,
    q_s, q_r, o_s, o_r, t_s, t_r, a_s, a_r, b_s, b_r, ready,
):
    z = lax.axis_index("ctx")
    me = lax.axis_index("mp")
    core = lax.rem(me, 2)
    chip = me // 2
    chips = m // 2
    partner = chip * 2 + 1 - core
    pivot = n // 3
    slots = n - pivot
    rows = xb.shape[1]
    heads = gown.shape[0]
    groups = lf_ref.shape[0]
    per_tile = groups // heads
    width = HD // per_tile
    tap_count = lf_ref.shape[1]
    short = sf_ref.shape[0]
    span = min(3, slots) * rows
    query_groups = qbuf.shape[1] // span
    cols = out_ref.shape[1]
    channels = xb.shape[2]
    own = jnp.minimum(z, pivot)

    def remote(src, dst, ss, rs, axis, target):
        return pltpu.make_async_remote_copy(
            src_ref=src, dst_ref=dst, send_sem=ss, recv_sem=rs,
            device_id={axis: target}, device_id_type=MESH)

    barrier = pltpu.get_barrier_semaphore()
    hops = max(pivot, n - 1 - pivot)
    relayed = hops == 2

    def there(d, side):
        return lax.rem(chip + d, chips) * 2 + side

    pl.semaphore_signal(barrier, inc=1, device_id={"mp": partner}, device_id_type=MESH)
    for d in range(1, chips):
        pl.semaphore_signal(barrier, inc=1, device_id={"mp": there(d, core)}, device_id_type=MESH)
    count = jnp.int32(chips)
    beside = jnp.int32(0)
    for other in range(n):
        low, high = jnp.minimum(z, other), jnp.maximum(z, other)
        near = high == low + 1
        beside = beside + near.astype(jnp.int32)
        talks = near
        if not relayed:
            talks = (low != high) & (near | (high <= pivot) | (low >= pivot))
        count = count + talks.astype(jnp.int32)

        @pl.when(talks)
        def _():
            pl.semaphore_signal(barrier, inc=1, device_id={"ctx": other}, device_id_type=MESH)

    local_x = pltpu.make_async_copy(x_hbm, xb, xsem)
    local_x.start()
    small = [pltpu.make_async_copy(a, b, psem.at[i]) for i, (a, b) in enumerate(
        ((sf_hbm, sf_ref), (lf_hbm, lf_ref), (skip_hbm, skip_ref)))]
    for c in small:
        c.start()
    local_k, local_q = [], []
    for h in range(heads):
        part = pl.ds(h * HD, HD)
        local_k.append(pltpu.make_async_copy(k_hbm.at[:, part], kbuf.at[own, h], ksem.at[h]))
        local_q.append(pltpu.make_async_copy(q_hbm.at[:, part], qbuf.at[h, pl.ds(0, rows)], qsem.at[h]))
    for c in local_k + local_q:
        c.start()
    local_w = pltpu.make_async_copy(w_hbm, wv, wsem)
    local_w.start()

    local_x.wait()
    for j in range(3):
        rim_out[2 * j:2 * j + 2, :] = xb[j, rows - 2:rows, :]

    @pl.when(z == 0)
    def _():
        rim_in[...] = jnp.zeros_like(rim_in)
        gprev[...] = jnp.zeros_like(gprev)

    pl.semaphore_wait(barrier, count)
    if relayed:
        inner = (z > 0) & (z < n - 1)
        for step in (-1, 1):
            @pl.when(inner)
            def _():
                pl.semaphore_signal(
                    ready, inc=1, device_id={"ctx": jnp.clip(z + step, 0, n - 1)}, device_id_type=MESH)

    up = jnp.minimum(z + 1, n - 1)
    rim = remote(rim_out, rim_in, rim_s, rim_r, "ctx", up)

    def gate(h):
        return remote(gown.at[h], gprev.at[h], gate_s.at[h], gate_r.at[h], "ctx", up)

    @pl.when(z < n - 1)
    def _():
        rim.start()

    for c in local_k + local_q:
        c.wait()

    def each_query(h, act, least=1, most=None):
        for other in range(pivot, n - 1):
            @pl.when((other + least <= z) & (z <= other + (most or n)))
            def _():
                act(remote(
                    qbuf.at[h, pl.ds(0, rows)],
                    qbuf.at[h, pl.ds(pl.multiple_of((z - other) * rows, rows), rows)],
                    q_s.at[other - pivot, h], q_r.at[z - other, h], "ctx", other))

    def each_key(h, act):
        for other in range(1, pivot + 1):
            @pl.when((other > z) & (z < pivot))
            def _():
                act(remote(kbuf.at[own, h], kbuf.at[own, h], k_s.at[other, h], k_r.at[own, h], "ctx", other))

    def each_value(h, act):
        for other in range(1, pivot + 1):
            @pl.when((other > z) & (z < pivot))
            def _():
                act(remote(vbuf.at[own, h], vbuf.at[own, h], v_s.at[other, h], v_r.at[own, h], "ctx", other))

    early = min(2, heads)
    ahead = min(4, heads)
    for h in range(early):
        each_key(h, lambda c: c.start())

    for h in range(early):
        each_query(h, lambda c: c.start(), 1, 1)

    @pl.when(z > 0)
    def _():
        rim.wait_recv()

    for c in small:
        c.wait()
    row = lax.broadcasted_iota(jnp.int32, (rows, HD), 0)

    @pl.loop(0, heads)
    def _(h):
        part = pl.ds(pl.multiple_of(h * HD, HD), HD)
        edge = rim_in[:, part].astype(F32)
        feats = []
        for j in range(3):
            x = xb[j, :, part].astype(F32)
            last = edge[2 * j + 1:2 * j + 2]
            x1 = jnp.where(row == 0, last, pltpu.roll(x, 1, 0))
            x2 = jnp.where(row == 0, edge[2 * j:2 * j + 1],
                           jnp.where(row == 1, last, pltpu.roll(x, 2, 0)))
            total = sf_ref[0, j:j + 1, part].astype(F32) * x
            total = total + sf_ref[1, j:j + 1, part].astype(F32) * x1
            feats.append(total + sf_ref[2, j:j + 1, part].astype(F32) * x2)
        f0[h] = feats[0]
        gown[h] = (feats[1] * feats[2]).astype(BF)

        @pl.when((z < n - 1) & ((z >= pivot) | (h < ahead)))
        def _():
            gate(h).start()

    if relayed:
        pl.semaphore_wait(ready, (z > 1).astype(jnp.int32) + (z < n - 2).astype(jnp.int32))

    @pl.loop(0, heads)
    def _(h):
        each_query(h, lambda c: c.start(), 2)

        @pl.when(h >= early)
        def _():
            each_query(h, lambda c: c.start(), 1, 1)

    flip = (lax.broadcasted_iota(jnp.int32, (tap_count, 2 * rows), 0)
            + lax.broadcasted_iota(jnp.int32, (tap_count, 2 * rows), 1)) == rows
    based = dot(lf_ref[...], flip.astype(BF))
    for g in range(groups):
        wide = jnp.broadcast_to(based[g:g + 1], (rows, 2 * rows))
        taps[g] = pltpu.roll(wide, 0, 1, stride=1, stride_axis=0).astype(BF)
    acc[...] = jnp.zeros_like(acc)

    lane = lax.broadcasted_iota(jnp.int32, (rows, HD), 1) // width

    def mix(h):
        @pl.when((z < pivot) & (h >= ahead))
        def _():
            gate(h).start()

        @pl.when(z > 0)
        def _():
            gate(h).wait_recv()

        mine = gown[h]
        both = jnp.concatenate([gprev[h], mine], axis=0)
        filt = jnp.zeros((rows, HD), F32)
        for g in range(per_tile):
            filt = jnp.where(lane == g, dot(taps[h * per_tile + g], both), filt)
        part = pl.ds(pl.multiple_of(h * HD, HD), HD)
        val = f0[h] * (filt + skip_ref[:, part] * mine.astype(F32))
        vbuf[own, h] = val.T.astype(BF)

        @pl.when(h >= early)
        def _():
            each_key(h, lambda c: c.start())

        each_value(h, lambda c: c.start())

    scale = HD ** -0.5
    krow = lax.broadcasted_iota(jnp.int32, (rows, span), 0)
    kcol = lax.broadcasted_iota(jnp.int32, (rows, span), 1)

    def each_part(h, act):
        for s in range(1, slots):
            @pl.when((z >= pivot) & (z + s < n))
            def _():
                act(s,
                    remote(sbuf.at[s - 1, h], pbuf.at[z - pivot, h],
                           o_s.at[s - 1, h], o_r.at[z - pivot, h], "ctx", z + s),
                    remote(sstat.at[s - 1, h], pstat.at[z - pivot, h],
                           t_s.at[s - 1, h], t_r.at[z - pivot, h], "ctx", z + s))

    def hand_over(h):
        def act(s, o, t):
            gi, at = (s * rows) // span, (s * rows) % span
            mm = mst[h, gi, :, at:at + rows]
            ll = lst[h, gi, :, at:at + rows]
            aa = ast[h, gi, :, at:at + rows]
            sbuf[s - 1, h] = (aa * (1.0 / ll[0:1])).astype(BF)
            sstat[s - 1, h] = mm[0:1] + jnp.log(ll[0:1])
            o.start()
            t.start()
        each_part(h, act)

    def own_keys(h):
        for s in range(1, slots):
            @pl.when((z >= pivot) & (z + s < n))
            def _():
                remote(qbuf.at[h, pl.ds(0, rows)], qbuf.at[h, pl.ds(s * rows, rows)],
                       q_s.at[0, h], q_r.at[s, h], "ctx", jnp.minimum(z + s, n - 1)).wait_recv()

        for gi in range(query_groups):
            q = qbuf[h, gi * span:(gi + 1) * span]
            s = dot(kbuf[own, h], q, 1, 1) * scale
            s = jnp.where(krow <= kcol + gi * span, s, NEG)
            mx = jnp.max(s, axis=0, keepdims=True)
            p = jnp.exp(s - mx)
            mst[h, gi] = jnp.broadcast_to(mx, (8, span))
            lst[h, gi] = jnp.broadcast_to(jnp.sum(p, axis=0, keepdims=True), (8, span))
            ast[h, gi] = dot(vbuf[own, h], p.astype(BF))

    @pl.when(z > pivot)
    def _():
        @pl.loop(0, heads)
        def _(h):
            mix(h)
            own_keys(h)
            hand_over(h)

    def one_head(h):
        @pl.when(z <= pivot)
        def _():
            mix(h)
            own_keys(h)

        @pl.loop(0, jnp.where(z <= pivot, z, 0))
        def _(j):
            remote(kbuf.at[j, h], kbuf.at[j, h], k_s.at[0, 0], k_r.at[j, h], "ctx", j).wait_recv()
            remote(vbuf.at[j, h], vbuf.at[j, h], v_s.at[0, 0], v_r.at[j, h], "ctx", j).wait_recv()
            for gi in range(query_groups):
                q = qbuf[h, gi * span:(gi + 1) * span]
                s = dot(kbuf[j, h], q, 1, 1) * scale
                old = mst[h, gi, 0:1]
                mx = jnp.maximum(old, jnp.max(s, axis=0, keepdims=True))
                p = jnp.exp(s - mx)
                fade = jnp.exp(old - mx)
                mst[h, gi] = jnp.broadcast_to(mx, (8, span))
                lst[h, gi] = jnp.broadcast_to(
                    lst[h, gi, 0:1] * fade + jnp.sum(p, axis=0, keepdims=True), (8, span))
                ast[h, gi] = ast[h, gi] * fade + dot(vbuf[j, h], p.astype(BF))

        @pl.when(z == pivot)
        def _():
            hand_over(h)

        @pl.loop(0, jnp.maximum(z - pivot, 0))
        def _(j):
            remote(sbuf.at[0, 0], pbuf.at[j, h], o_s.at[0, 0], o_r.at[j, h], "ctx", j + pivot).wait_recv()
            remote(sstat.at[0, 0], pstat.at[j, h], t_s.at[0, 0], t_r.at[j, h], "ctx", j + pivot).wait_recv()
            old = mst[h, 0, :, 0:rows]
            lse = pstat[j, h]
            mx = jnp.maximum(old, lse)
            fade, gain = jnp.exp(old - mx), jnp.exp(lse - mx)
            mst[h, 0, :, 0:rows] = mx
            lst[h, 0, :, 0:rows] = lst[h, 0, :, 0:rows] * fade + gain
            ast[h, 0, :, 0:rows] = ast[h, 0, :, 0:rows] * fade[0:1] + pbuf[j, h].astype(F32) * gain[0:1]

        done = ast[h, 0, :, 0:rows] * (1.0 / lst[h, 0, 0:1, 0:rows])
        return done.T.astype(BF)

    @pl.loop(0, heads // 2)
    def _(c):
        att[c, :, 0:HD] = one_head(2 * c)
        att[c, :, HD:2 * HD] = one_head(2 * c + 1)

        @pl.when(c == 0)
        def _():
            local_w.wait()

        @pl.when(c < heads // 2 - 1)
        def _():
            lhs = att[c]

            @pl.loop(0, m)
            def _(b):
                at = pl.ds(pl.multiple_of(b * cols, cols), cols)
                acc[b] += dot(lhs, wv[pl.ds(pl.multiple_of(c * 2 * HD, 2 * HD), 2 * HD), at])

    pieces = 4
    piece = cols // pieces

    def across(d, i):
        return remote(s1.at[d, i], r1.at[d, i], a_s.at[d, i], a_r.at[d, i], "mp", partner)

    def along(d, i):
        there = lax.rem(chip + d, chips) * 2 + core
        return remote(s2.at[d, i], r2.at[d, i], b_s.at[d, i], b_r.at[d, i], "mp", there)

    last = att[heads // 2 - 1]

    def summed(b, i):
        at = pl.ds(pl.multiple_of(b * cols + i * piece, piece), piece)
        return acc[b, :, i * piece:(i + 1) * piece] + dot(last, wv[channels - 2 * HD:, at])

    def block(d, side):
        return lax.rem(chip + d, chips) * 2 + side

    order = [d % chips for d in range(1, chips + 1)]
    for d in order:
        for i in range(pieces):
            s1[d, i] = summed(block(d, 1 - core), i).astype(BF)
            across(d, i).start()
    for d in range(1, chips):
        for i in range(pieces):
            total = summed(block(d, core), i)
            across(d, i).wait_recv()
            s2[d, i] = (total + r1[d, i].astype(F32)).astype(BF)
            along(d, i).start()
    for i in range(pieces):
        acc[me, :, i * piece:(i + 1) * piece] = summed(me, i)
    for i in range(pieces):
        across(0, i).wait_recv()
        acc[me, :, i * piece:(i + 1) * piece] += r1[0, i].astype(F32)
    for i in range(pieces):
        total = acc[me, :, i * piece:(i + 1) * piece]
        for d in range(1, chips):
            along(d, i).wait_recv()
            total = total + r2[d, i].astype(F32)
        out_ref[:, i * piece:(i + 1) * piece] = total.astype(BF)

    for i in range(pieces):
        for d in range(chips):
            across(d, i).wait_send()
        for d in range(1, chips):
            along(d, i).wait_send()

    @pl.when(z < n - 1)
    def _():
        rim.wait_send()

    @pl.loop(0, heads)
    def _(h):
        def ended(s, o, t):
            o.wait_send()
            t.wait_send()
        @pl.when(z < n - 1)
        def _():
            gate(h).wait_send()

        each_query(h, lambda c: c.wait_send())
        each_key(h, lambda c: c.wait_send())
        each_value(h, lambda c: c.wait_send())
        each_part(h, ended)


def per_device(n, m, inputs, short_filter, long_filter, skip_gain, queries, key_rows, out_weight):
    rows, _, channels = inputs.shape
    heads = channels // HD
    groups = long_filter.shape[0]
    total = out_weight.shape[1]
    cols = total // m
    chips = m // 2
    pivot = n // 3
    slots = n - pivot
    batch = min(3, slots)
    padded = -(-slots // batch) * batch
    span = batch * rows
    gq = padded // batch
    parts = max(slots - 1, 1)
    vm = pltpu.VMEM
    dma = pltpu.SemaphoreType.DMA
    scratch = [
        vm(short_filter.shape, BF), vm(long_filter.shape, BF), vm((1, channels), F32), dma((3,)),
        vm((3, rows, channels), BF), vm((16, channels), BF), vm((16, channels), BF),
        vm((heads, rows, HD), F32), vm((heads, rows, HD), BF), vm((heads, rows, HD), BF),
        vm((groups, rows, 2 * rows), BF),
        vm((pivot + 1, heads, rows, HD), BF), vm((pivot + 1, heads, HD, rows), BF),
        vm((heads, padded * rows, HD), BF),
        vm((heads, gq, 8, span), F32), vm((heads, gq, 8, span), F32), vm((heads, gq, HD, span), F32),
        vm((parts, heads, HD, rows), BF), vm((parts, heads, 1, rows), F32),
        vm((parts, heads, HD, rows), BF), vm((parts, heads, 1, rows), F32),
        vm((heads // 2, rows, 2 * HD), BF), vm((channels, total), BF), vm((m, rows, cols), F32),
    ] + [vm((chips, 4, rows, cols // 4), BF)] * 4 + [
        dma, dma((heads,)), dma((heads,)), dma, dma, dma, dma((heads,)), dma((heads,)),
    ] + [dma((pivot + 1, heads))] * 4 + [dma((slots, heads))] * 2 + [
        dma((parts, heads)), dma((parts, heads)), dma((parts, heads)), dma((parts, heads)),
    ] + [dma((chips, 4))] * 4 + [pltpu.SemaphoreType.REGULAR]
    in_vmem = pl.BlockSpec(memory_space=pltpu.VMEM)
    in_hbm = pl.BlockSpec(memory_space=pl.ANY)
    return pl.pallas_call(
        functools.partial(kernel, n, m),
        out_shape=pltpu.VMEM((rows, cols), BF),
        in_specs=[in_hbm] * 7,
        out_specs=in_vmem,
        scratch_shapes=scratch,
        compiler_params=pltpu.CompilerParams(
            collective_id=0, has_side_effects=True, vmem_limit_bytes=60 * 2**20),
    )(inputs.transpose(1, 0, 2), short_filter, long_filter, skip_gain[None], queries, key_rows, out_weight)


def solution(mesh):
    placed = (
        P(("parts", "ctx"), None, "mp"),
        P(None, None, "mp"),
        P("mp", None),
        P("mp"),
        P(("parts", "ctx"), "mp"),
        P(("parts", "ctx"), "mp"),
        P("mp", None),
    )
    return jax.shard_map(
        functools.partial(per_device, mesh.shape["ctx"], mesh.shape["mp"]),
        mesh=mesh, in_specs=placed, out_specs=P(("parts", "ctx"), "mp"), check_vma=False)
```

```python
import functools

import jax
import jax.numpy as jnp
from jax import lax
from jax.experimental import pallas as pl
from jax.experimental.pallas import tpu as pltpu
from jax.sharding import PartitionSpec as P

HD = 128
LATE = 0
MESH = pl.DeviceIdType.MESH
NEG = -1e30
F32 = jnp.float32
BF = jnp.bfloat16


def dot(a, b, ca=1, cb=0):
    return lax.dot_general(a, b, (((ca,), (cb,)), ((), ())), preferred_element_type=F32)


def kernel(
    n, m, parts, late, x_hbm, sf_hbm, lf_hbm, skip_hbm, q_hbm, k_hbm, w_hbm, out_ref,
    sf_ref, lf_ref, skip_ref, psem, xb, rim_out, rim_in, f0, gown, gprev, taps, kbuf, vbuf, qbuf, mst, lst, ast,
    sbuf, sstat, pbuf, pstat, att, pat, wv, acc, s2, r2, wl, atl,
    xsem, qsem, ksem, wsem, rim_s, rim_r, gate_s, gate_r, k_s, k_r, v_s, v_r,
    q_s, q_r, o_s, o_r, t_s, t_r, b_s, b_r, ready,
    pw_s, pw_r, pat_s, pat_r, wx_s, wx_r, wy_s, wy_r, at_s, at_r,
):
    z = lax.axis_index("ctx")
    me = lax.axis_index("mp")
    part_at = lax.axis_index("parts")
    core = lax.rem(me, 2)
    chip = me // 2
    chips = m // 2
    partner = chip * 2 + 1 - core
    pivot = n // 3
    slots = n - pivot
    rows = xb.shape[1]
    heads = gown.shape[0]
    groups = lf_ref.shape[0]
    per_tile = groups // heads
    width = HD // per_tile
    tap_count = lf_ref.shape[1]
    span = min(3, slots) * rows
    query_groups = qbuf.shape[1] // span
    cols = out_ref.shape[1]
    own = jnp.minimum(z, pivot)
    sure = heads - late
    joint = pivot == 1 and query_groups == 1

    def remote(src, dst, ss, rs, axis, target):
        return pltpu.make_async_remote_copy(
            src_ref=src, dst_ref=dst, send_sem=ss, recv_sem=rs,
            device_id={axis: target}, device_id_type=MESH)

    def there(d, side):
        return lax.rem(chip + d, chips) * 2 + side

    beyond = [(d, side) for d in range(1, chips) for side in range(2)]

    def at_side(d, side):
        return there(d, jnp.abs(core - side))

    barrier = pltpu.get_barrier_semaphore()
    hops = max(pivot, n - 1 - pivot)
    relayed = hops == 2
    pl.semaphore_signal(barrier, inc=1, device_id={"mp": partner}, device_id_type=MESH)
    for d, side in beyond:
        if late or side == 0:
            pl.semaphore_signal(barrier, inc=1, device_id={"mp": at_side(d, side)}, device_id_type=MESH)
    for d in range(1, parts):
        if late:
            pl.semaphore_signal(
                barrier, inc=1, device_id={"parts": lax.rem(part_at + d, parts)}, device_id_type=MESH)
    count = jnp.int32(m - 1 + parts - 1 if late else chips)
    for other in range(n):
        low, high = jnp.minimum(z, other), jnp.maximum(z, other)
        talks = high == low + 1
        if not relayed:
            talks = (low != high) & (talks | (high <= pivot) | (low >= pivot))
        count = count + talks.astype(jnp.int32)

        @pl.when(talks)
        def _():
            pl.semaphore_signal(barrier, inc=1, device_id={"ctx": other}, device_id_type=MESH)

    local_k, local_q = [], []
    for h in range(heads):
        part = pl.ds(h * HD, HD)
        local_k.append(pltpu.make_async_copy(k_hbm.at[:, part], kbuf.at[own, h], ksem.at[h]))
        local_q.append(pltpu.make_async_copy(q_hbm.at[:, part], qbuf.at[h, pl.ds(0, rows)], qsem.at[h]))
    for c in local_k[:2] + local_q[:2]:
        c.start()
    local_x = pltpu.make_async_copy(x_hbm, xb, xsem)
    local_x.start()
    small = [pltpu.make_async_copy(a, b, psem.at[i]) for i, (a, b) in enumerate(
        ((sf_hbm, sf_ref), (lf_hbm, lf_ref), (skip_hbm, skip_ref)))]
    for c in small:
        c.start()
    for c in local_k[2:] + local_q[2:]:
        c.start()

    local_x.wait()
    for j in range(3):
        rim_out[2 * j:2 * j + 2, :] = xb[j, rows - 2:rows, :]

    @pl.when(z == 0)
    def _():
        gprev[...] = jnp.zeros_like(gprev)

    pl.semaphore_wait(barrier, count)
    if relayed:
        inner = (z > 0) & (z < n - 1)
        for step in (-1, 1):
            @pl.when(inner)
            def _():
                pl.semaphore_signal(
                    ready, inc=1, device_id={"ctx": jnp.clip(z + step, 0, n - 1)}, device_id_type=MESH)

    up = jnp.minimum(z + 1, n - 1)
    rim = remote(rim_out, rim_in, rim_s, rim_r, "ctx", up)

    def gate(h):
        return remote(gown.at[h], gprev.at[h], gate_s.at[h], gate_r.at[h], "ctx", up)

    @pl.when(z < n - 1)
    def _():
        rim.start()

    def each_query(h, act, least=1, most=None):
        for other in range(pivot, n - 1):
            @pl.when((other + least <= z) & (z <= other + (most or n)))
            def _():
                act(remote(
                    qbuf.at[h, pl.ds(0, rows)],
                    qbuf.at[h, pl.ds(pl.multiple_of((z - other) * rows, rows), rows)],
                    q_s.at[other - pivot, h], q_r.at[z - other, h], "ctx", other))

    def each_key(h, act):
        for other in range(1, pivot + 1):
            @pl.when((other > z) & (z < pivot))
            def _():
                act(remote(kbuf.at[own, h], kbuf.at[own, h], k_s.at[other, h], k_r.at[own, h], "ctx", other))

    def each_value(h, act):
        for other in range(1, pivot + 1):
            @pl.when((other > z) & (z < pivot))
            def _():
                act(remote(vbuf.at[own, h], vbuf.at[own, h], v_s.at[other, h], v_r.at[own, h], "ctx", other))

    early = min(2, heads)
    steady = max(early, heads - 2)
    for h in range(early):
        local_k[h].wait()
        local_q[h].wait()
        each_key(h, lambda c: c.start())
        each_query(h, lambda c: c.start(), 1, 1)

    for c in small:
        c.wait()

    def featured(h, size, edge):
        part = pl.ds(pl.multiple_of(h * HD, HD), HD)
        row = lax.broadcasted_iota(jnp.int32, (size, HD), 0)
        feats = []
        for j in range(3):
            x = xb[j, 0:size, part].astype(F32)
            last = edge[2 * j + 1:2 * j + 2] if edge is not None else 0.0
            prior = edge[2 * j:2 * j + 1] if edge is not None else 0.0
            x1 = jnp.where(row == 0, last, pltpu.roll(x, 1, 0))
            x2 = jnp.where(row == 0, prior, jnp.where(row == 1, last, pltpu.roll(x, 2, 0)))
            total = sf_ref[0, j:j + 1, part].astype(F32) * x
            total = total + sf_ref[1, j:j + 1, part].astype(F32) * x1
            feats.append(total + sf_ref[2, j:j + 1, part].astype(F32) * x2)
        f0[h, 0:size] = feats[0]
        gown[h, 0:size] = (feats[1] * feats[2]).astype(BF)

    @pl.loop(0, heads)
    def _(h):
        featured(h, rows, None)

        @pl.when((z == 0) & (h < early))
        def _():
            gate(h).start()

    for c in local_k[early:] + local_q[early:]:
        c.wait()

    @pl.when(z > 0)
    def _():
        rim.wait_recv()

    @pl.loop(0, heads)
    def _(h):
        @pl.when(z > 0)
        def _():
            featured(h, 16, rim_in[:, pl.ds(pl.multiple_of(h * HD, HD), HD)].astype(F32))

        @pl.when((z > 0) & (z < n - 1) & ((z >= pivot) | (h < early)))
        def _():
            gate(h).start()

    if relayed:
        pl.semaphore_wait(ready, (z > 1).astype(jnp.int32) + (z < n - 2).astype(jnp.int32))

    @pl.loop(0, heads)
    def _(h):
        each_query(h, lambda c: c.start(), 2)

        @pl.when(h >= early)
        def _():
            each_query(h, lambda c: c.start(), 1, 1)

    half = heads // 2
    local_w, over_core = [], []
    for g in range(2):
        for d in range(chips):
            def columns(side):
                return w_hbm.at[pl.ds(g * half, half), :, pl.ds(pl.multiple_of(there(d, side) * cols, cols), cols)]

            def place(lo):
                return wv.at[pl.ds(g * half, half), pl.ds(lo, HD), pl.ds(d * cols, cols)]
            local_w.append(pltpu.make_async_copy(columns(core), place(0), wsem.at[g, d]))
            over_core.append(remote(columns(1 - core), place(HD), pw_s.at[g, d], pw_r.at[g, d], "mp", partner))
    for a, b in zip(local_w, over_core):
        a.start()
        b.start()

    slab = late // parts
    bit = HD // 2
    chunks = [(d, side, e, i) for d, side in beyond for e in range(slab) for i in range(2)]

    def late_part(src, owner, e, i):
        return wl.at[src, owner * slab + e, pl.ds(i * bit, bit)]

    def over_x(src, b, e, i):
        return remote(
            w_hbm.at[sure + part_at * slab + e, pl.ds(i * bit, bit), pl.ds(pl.multiple_of(b * cols, cols), cols)],
            late_part(src, part_at, e, i), wx_s.at[b, e, i], wx_r.at[src, e, i], "mp", b)

    def over_y(src, owner, e, i, d):
        ref = late_part(src, owner, e, i)
        return remote(ref, ref, wy_s.at[d, src, e, i], wy_r.at[owner, src, e, i],
                      "parts", lax.rem(part_at + d, parts))

    for d, side, e, i in chunks:
        over_x(me, at_side(d, side), e, i).start()

    def swap(d, side, e, i):
        src = at_side(d, side)
        over_x(src, src, e, i).wait_recv()
        for k in range(1, parts):
            over_y(src, part_at, e, i, k).start()

    flip = (lax.broadcasted_iota(jnp.int32, (tap_count, 2 * rows), 0)
            + lax.broadcasted_iota(jnp.int32, (tap_count, 2 * rows), 1)) == rows
    based = dot(lf_ref[...], flip.astype(BF))
    for g in range(groups):
        wide = jnp.broadcast_to(based[g:g + 1], (rows, 2 * rows))
        taps[g] = pltpu.roll(wide, 0, 1, stride=1, stride_axis=0).astype(BF)
    acc[...] = jnp.zeros_like(acc)

    lane = lax.broadcasted_iota(jnp.int32, (rows, HD), 1) // width

    def mix(h):
        @pl.when(z > 0)
        def _():
            gate(h).wait_recv()

        mine = gown[h]
        both = jnp.concatenate([gprev[h], mine], axis=0)
        filt = jnp.zeros((rows, HD), F32)
        for g in range(per_tile):
            filt = jnp.where(lane == g, dot(taps[h * per_tile + g], both), filt)
        part = pl.ds(pl.multiple_of(h * HD, HD), HD)
        val = f0[h] * (filt + skip_ref[:, part] * mine.astype(F32))
        vbuf[own, h] = val.T.astype(BF)

    def key_and_gate(h):
        each_key(h, lambda c: c.start())

        @pl.when(z < n - 1)
        def _():
            gate(h).start()

    @pl.when(z < pivot)
    def _():
        @pl.loop(0, heads)
        def _(h):
            @pl.when(h >= steady)
            def _():
                key_and_gate(h)

            mix(h)
            each_value(h, lambda c: c.start())

            @pl.when(h + early < steady)
            def _():
                key_and_gate(h + early)

    scale = HD ** -0.5
    krow = lax.broadcasted_iota(jnp.int32, (rows, span), 0)
    kcol = lax.broadcasted_iota(jnp.int32, (rows, span), 1)

    def each_part(h, act):
        for s in range(1, slots):
            @pl.when((z >= pivot) & (z + s < n))
            def _():
                act(s,
                    remote(sbuf.at[s - 1, h], pbuf.at[z - pivot, h],
                           o_s.at[s - 1, h], o_r.at[z - pivot, h], "ctx", z + s),
                    remote(sstat.at[s - 1, h], pstat.at[z - pivot, h],
                           t_s.at[s - 1, h], t_r.at[z - pivot, h], "ctx", z + s))

    def hand_over(h):
        def act(s, o, t):
            gi, at = (s * rows) // span, (s * rows) % span
            mm = mst[h, gi, :, at:at + rows]
            ll = lst[h, gi, :, at:at + rows]
            aa = ast[h, gi, :, at:at + rows]
            sbuf[s - 1, h] = (aa * (1.0 / ll[0:1])).astype(BF)
            sstat[s - 1, h] = mm[0:1] + jnp.log(ll[0:1])
            o.start()
            t.start()
        each_part(h, act)

    def queries_in(h):
        for s in range(1, slots):
            @pl.when((z >= pivot) & (z + s < n))
            def _():
                remote(qbuf.at[h, pl.ds(0, rows)], qbuf.at[h, pl.ds(s * rows, rows)],
                       q_s.at[0, h], q_r.at[s, h], "ctx", jnp.minimum(z + s, n - 1)).wait_recv()

    def own_keys(h):
        queries_in(h)
        for gi in range(query_groups):
            q = qbuf[h, gi * span:(gi + 1) * span]
            s = dot(kbuf[own, h], q, 1, 1) * scale
            s = jnp.where(krow <= kcol + gi * span, s, NEG)
            mx = jnp.max(s, axis=0, keepdims=True)
            p = jnp.exp(s - mx)
            mst[h, gi] = jnp.broadcast_to(mx, (8, span))
            lst[h, gi] = jnp.broadcast_to(jnp.sum(p, axis=0, keepdims=True), (8, span))
            ast[h, gi] = dot(vbuf[own, h], p.astype(BF))

    def key_in(j, h):
        return remote(kbuf.at[j, h], kbuf.at[j, h], k_s.at[0, 0], k_r.at[j, h], "ctx", j)

    def value_in(j, h):
        return remote(vbuf.at[j, h], vbuf.at[j, h], v_s.at[0, 0], v_r.at[j, h], "ctx", j)

    @pl.when(z > pivot)
    def _():
        @pl.loop(0, heads)
        def _(h):
            mix(h)
            own_keys(h)
            hand_over(h)

    def finished(h):
        att[h] = (ast[h, 0, :, 0:rows] * (1.0 / lst[h, 0, 0:1, 0:rows])).T.astype(BF)

    def front(h):
        s = dot(kbuf[0, h], qbuf[h, 0:rows], 1, 1) * scale
        s = jnp.where(krow[:, 0:rows] <= kcol[:, 0:rows], s, NEG)
        p = jnp.exp(s - jnp.max(s, axis=0, keepdims=True))
        o = dot(vbuf[0, h], p.astype(BF)) * (1.0 / jnp.sum(p, axis=0, keepdims=True))
        att[h] = o.T.astype(BF)

    def hub(h):
        key_in(0, h).wait_recv()
        queries_in(h)
        s = dot(jnp.concatenate([kbuf[0, h], kbuf[1, h]], axis=0), qbuf[h], 1, 1) * scale
        krow2 = lax.broadcasted_iota(jnp.int32, (2 * rows, span), 0) - rows
        kcol2 = lax.broadcasted_iota(jnp.int32, (2 * rows, span), 1)
        s = jnp.where(krow2 <= kcol2, s, NEG)
        mx = jnp.max(s, axis=0, keepdims=True)
        p = jnp.exp(s - mx)
        total = jnp.sum(p, axis=0, keepdims=True)
        p = p.astype(BF)
        inv = 1.0 / total
        lse = mx + jnp.log(total)
        mix(h)
        value_in(0, h).wait_recv()
        o = dot(jnp.concatenate([vbuf[0, h], vbuf[1, h]], axis=1), p) * inv

        def act(s, c, t):
            at = slice(s * rows, (s + 1) * rows)
            sbuf[s - 1, h] = o[:, at].astype(BF)
            sstat[s - 1, h] = lse[:, at]
            c.start()
            t.start()
        each_part(h, act)
        att[h] = o[:, 0:rows].T.astype(BF)

    def rear(h):
        @pl.loop(0, jnp.maximum(z - pivot, 0))
        def _(j):
            remote(sbuf.at[0, 0], pbuf.at[j, h], o_s.at[0, 0], o_r.at[j, h], "ctx", j + pivot).wait_recv()
            remote(sstat.at[0, 0], pstat.at[j, h], t_s.at[0, 0], t_r.at[j, h], "ctx", j + pivot).wait_recv()
            old = mst[h, 0, :, 0:rows]
            lse = pstat[j, h]
            mx = jnp.maximum(old, lse)
            fade, gain = jnp.exp(old - mx), jnp.exp(lse - mx)
            mst[h, 0, :, 0:rows] = mx
            lst[h, 0, :, 0:rows] = lst[h, 0, :, 0:rows] * fade + gain
            ast[h, 0, :, 0:rows] = ast[h, 0, :, 0:rows] * fade[0:1] + pbuf[j, h].astype(F32) * gain[0:1]
        finished(h)

    def one_head(h):
        if joint:
            @pl.when(z < pivot)
            def _():
                front(h)

            @pl.when(z == pivot)
            def _():
                hub(h)
        else:
            @pl.when(z <= pivot)
            def _():
                @pl.when(z == pivot)
                def _():
                    mix(h)

                own_keys(h)

                @pl.loop(0, z)
                def _(j):
                    key_in(j, h).wait_recv()
                    value_in(j, h).wait_recv()
                    for gi in range(query_groups):
                        q = qbuf[h, gi * span:(gi + 1) * span]
                        s = dot(kbuf[j, h], q, 1, 1) * scale
                        old = mst[h, gi, 0:1]
                        mx = jnp.maximum(old, jnp.max(s, axis=0, keepdims=True))
                        p = jnp.exp(s - mx)
                        fade = jnp.exp(old - mx)
                        mst[h, gi] = jnp.broadcast_to(mx, (8, span))
                        lst[h, gi] = jnp.broadcast_to(
                            lst[h, gi, 0:1] * fade + jnp.sum(p, axis=0, keepdims=True), (8, span))
                        ast[h, gi] = ast[h, gi] * fade + dot(vbuf[j, h], p.astype(BF))

                @pl.when(z == pivot)
                def _():
                    hand_over(h)

                finished(h)

        @pl.when(z > pivot)
        def _():
            rear(h)

    def beside(h):
        return remote(att.at[h], pat.at[h], pat_s.at[h], pat_r.at[h], "mp", partner)

    def gathered(src, l, b):
        return remote(att.at[sure + l], atl.at[src, l], at_s.at[b, l], at_r.at[src, l], "mp", b)

    pieces = 4
    piece = cols // pieces

    def along(d, i):
        return remote(s2.at[d, i], r2.at[d, i], b_s.at[d, i], b_r.at[d, i], "mp", there(d, core))

    def weights_in(g):
        for d in range(chips):
            local_w[g * chips + d].wait()
            over_core[g * chips + d].wait_recv()

    def both_cores(h):
        beside(h).wait_recv()
        return jnp.concatenate([att[h], pat[h]], axis=1)

    def project(h, blocks):
        lhs = both_cores(h)
        for d in range(blocks):
            acc[d] += dot(lhs, wv[h, :, d * cols:(d + 1) * cols])

    @pl.loop(0, sure)
    def _(h):
        one_head(h)
        beside(h).start()

        @pl.when(h == 1)
        def _():
            weights_in(0)

        @pl.when(h == half)
        def _():
            weights_in(1)

        @pl.when(h > 0)
        def _():
            project(h - 1, chips)

        for k, chunk in enumerate(chunks):
            @pl.when(h == min(sure - 1, 1 + k * (sure - 1) // len(chunks)))
            def _():
                swap(*chunk)

    if half >= sure:
        weights_in(1)
    if sure < 2:
        weights_in(0)
    lhs = both_cores(sure - 1)
    for d in range(1, chips):
        for i in range(pieces):
            at = slice(i * piece, (i + 1) * piece)
            s2[d, i] = (acc[d, :, at] + dot(
                lhs, wv[sure - 1, :, d * cols + i * piece:d * cols + (i + 1) * piece])).astype(BF)
            along(d, i).start()
    acc[0] += dot(lhs, wv[sure - 1, :, 0:cols])

    @pl.loop(0, late)
    def _(l):
        one_head(sure + l)
        for d, side in beyond:
            gathered(me, l, at_side(d, side)).start()
        beside(sure + l).start()

        @pl.when(l > 0)
        def _():
            project(sure + l - 1, 1)

    if late:
        project(heads - 1, 1)
    for d, side, e, i in chunks:
        for k in range(1, parts):
            owner = lax.rem(part_at + parts - k, parts)
            over_y(at_side(d, side), owner, e, i, k).wait_recv()
    if late:
        for d, side in beyond:
            src = at_side(d, side)
            for l in range(late):
                gathered(src, l, src).wait_recv()
    for i in range(pieces):
        at = slice(i * piece, (i + 1) * piece)
        total = acc[0, :, at]
        if late:
            for d, side in beyond:
                src = at_side(d, side)
                lhs = jnp.concatenate([atl[src, l] for l in range(late)], axis=1)
                total = total + dot(lhs, wl[src, :, :, at].reshape(late * HD, piece))
        for d in range(1, chips):
            along(d, i).wait_recv()
            total = total + r2[d, i].astype(F32)
        out_ref[:, at] = total.astype(BF)

    for i in range(pieces):
        for d in range(1, chips):
            along(d, i).wait_send()
    for c in over_core:
        c.wait_send()
    for d, side, e, i in chunks:
        src = at_side(d, side)
        over_x(me, src, e, i).wait_send()
        for k in range(1, parts):
            over_y(src, part_at, e, i, k).wait_send()
    for l in range(late):
        for d, side in beyond:
            gathered(me, l, at_side(d, side)).wait_send()

    @pl.when(z < n - 1)
    def _():
        rim.wait_send()

    @pl.loop(0, heads)
    def _(h):
        def ended(s, o, t):
            o.wait_send()
            t.wait_send()
        beside(h).wait_send()

        @pl.when(z < n - 1)
        def _():
            gate(h).wait_send()

        each_query(h, lambda c: c.wait_send())
        each_key(h, lambda c: c.wait_send())
        each_value(h, lambda c: c.wait_send())
        each_part(h, ended)


def per_device(n, m, parts_n, inputs, short_filter, long_filter, skip_gain, queries, key_rows, out_weight):
    rows, _, channels = inputs.shape
    heads = channels // HD
    groups = long_filter.shape[0]
    total = out_weight.shape[1]
    cols = total // m
    chips = m // 2
    pivot = n // 3
    slots = n - pivot
    batch = min(3, slots)
    padded = -(-slots // batch) * batch
    span = batch * rows
    gq = padded // batch
    parts = max(slots - 1, 1)
    late = LATE if LATE % parts_n == 0 and heads > LATE + 1 else 0
    slab = max(late // parts_n, 1)
    vm = pltpu.VMEM
    dma = pltpu.SemaphoreType.DMA
    scratch = [
        vm(short_filter.shape, BF), vm(long_filter.shape, BF), vm((1, channels), F32), dma((3,)),
        vm((3, rows, channels), BF), vm((16, channels), BF), vm((16, channels), BF),
        vm((heads, rows, HD), F32), vm((heads, rows, HD), BF), vm((heads, rows, HD), BF),
        vm((groups, rows, 2 * rows), BF),
        vm((pivot + 1, heads, rows, HD), BF), vm((pivot + 1, heads, HD, rows), BF),
        vm((heads, padded * rows, HD), BF),
        vm((heads, gq, 8, span), F32), vm((heads, gq, 8, span), F32), vm((heads, gq, HD, span), F32),
        vm((parts, heads, HD, rows), BF), vm((parts, heads, 1, rows), F32),
        vm((parts, heads, HD, rows), BF), vm((parts, heads, 1, rows), F32),
        vm((heads, rows, HD), BF), vm((heads, rows, HD), BF),
        vm((heads, 2 * HD, chips * cols), BF), vm((chips, rows, cols), F32),
        vm((chips, 4, rows, cols // 4), BF), vm((chips, 4, rows, cols // 4), BF),
        vm((m, max(late, 1), HD, cols), BF), vm((m, max(late, 1), rows, HD), BF),
        dma, dma((heads,)), dma((heads,)), dma((2, chips)), dma, dma, dma((heads,)), dma((heads,)),
    ] + [dma((pivot + 1, heads))] * 4 + [dma((slots, heads))] * 2 + [
        dma((parts, heads)), dma((parts, heads)), dma((parts, heads)), dma((parts, heads)),
    ] + [dma((chips, 4))] * 2 + [pltpu.SemaphoreType.REGULAR] + [
        dma((2, chips)), dma((2, chips)), dma((heads,)), dma((heads,)),
        dma((m, slab, 2)), dma((m, slab, 2)), dma((parts_n, m, slab, 2)), dma((parts_n, m, slab, 2)),
        dma((m, max(late, 1))), dma((m, max(late, 1))),
    ]
    in_vmem = pl.BlockSpec(memory_space=pltpu.VMEM)
    in_hbm = pl.BlockSpec(memory_space=pl.ANY)
    return pl.pallas_call(
        functools.partial(kernel, n, m, parts_n, late),
        out_shape=pltpu.VMEM((rows, cols), BF),
        in_specs=[in_hbm] * 7,
        out_specs=in_vmem,
        scratch_shapes=scratch,
        compiler_params=pltpu.CompilerParams(
            collective_id=0, has_side_effects=True, vmem_limit_bytes=60 * 2**20),
    )(inputs.transpose(1, 0, 2), short_filter, long_filter, skip_gain[None], queries, key_rows,
      out_weight.reshape(heads, HD, total))


def solution(mesh):
    placed = (
        P(("parts", "ctx"), None, "mp"),
        P(None, None, "mp"),
        P("mp", None),
        P("mp"),
        P(("parts", "ctx"), "mp"),
        P(("parts", "ctx"), "mp"),
        P("mp", None),
    )
    return jax.shard_map(
        functools.partial(per_device, mesh.shape["ctx"], mesh.shape["mp"], mesh.shape["parts"]),
        mesh=mesh, in_specs=placed, out_specs=P(("parts", "ctx"), "mp"), check_vma=False)
```

```python
import functools

import jax
import jax.numpy as jnp
from jax import lax
from jax.experimental import pallas as pl
from jax.experimental.pallas import tpu as pltpu
from jax.sharding import PartitionSpec as P

HD = 128
LATE = 0
MESH = pl.DeviceIdType.MESH
NEG = -1e30
F32 = jnp.float32
BF = jnp.bfloat16


def dot(a, b, ca=1, cb=0):
    return lax.dot_general(a, b, (((ca,), (cb,)), ((), ())), preferred_element_type=F32)


def kernel(
    n, m, parts, late, x_hbm, sf_hbm, lf_hbm, skip_hbm, q_hbm, k_hbm, w_hbm, out_ref,
    sf_ref, lf_ref, skip_ref, psem, xb, rim_out, rim_in, f0, gown, gprev, taps, kbuf, vbuf, qbuf, mst, lst, ast,
    sbuf, sstat, pbuf, pstat, att, pat, wv, acc, s2, r2, wl, atl,
    xsem, qsem, ksem, wsem, rim_s, rim_r, gate_s, gate_r, k_s, k_r, v_s, v_r,
    q_s, q_r, o_s, o_r, t_s, t_r, b_s, b_r, ready,
    pw_s, pw_r, pat_s, pat_r, wx_s, wx_r, wy_s, wy_r, at_s, at_r,
):
    z = lax.axis_index("ctx")
    me = lax.axis_index("mp")
    part_at = lax.axis_index("parts")
    core = lax.rem(me, 2)
    chip = me // 2
    chips = m // 2
    partner = chip * 2 + 1 - core
    pivot = n // 3
    slots = n - pivot
    rows = xb.shape[1]
    heads = gown.shape[0]
    groups = lf_ref.shape[0]
    per_tile = groups // heads
    width = HD // per_tile
    tap_count = lf_ref.shape[1]
    span = min(3, slots) * rows
    query_groups = qbuf.shape[1] // span
    cols = out_ref.shape[1]
    own = jnp.minimum(z, pivot)
    sure = heads - late
    joint = pivot == 1 and query_groups == 1

    def remote(src, dst, ss, rs, axis, target):
        return pltpu.make_async_remote_copy(
            src_ref=src, dst_ref=dst, send_sem=ss, recv_sem=rs,
            device_id={axis: target}, device_id_type=MESH)

    def there(d, side):
        return lax.rem(chip + d, chips) * 2 + side

    beyond = [(d, side) for d in range(1, chips) for side in range(2)]

    def at_side(d, side):
        return there(d, jnp.abs(core - side))

    barrier = pltpu.get_barrier_semaphore()
    hops = max(pivot, n - 1 - pivot)
    relayed = hops == 2
    pl.semaphore_signal(barrier, inc=1, device_id={"mp": partner}, device_id_type=MESH)
    for d, side in beyond:
        if late or side == 0:
            pl.semaphore_signal(barrier, inc=1, device_id={"mp": at_side(d, side)}, device_id_type=MESH)
    for d in range(1, parts):
        if late:
            pl.semaphore_signal(
                barrier, inc=1, device_id={"parts": lax.rem(part_at + d, parts)}, device_id_type=MESH)
    count = jnp.int32(m - 1 + parts - 1 if late else chips)
    for other in range(n):
        low, high = jnp.minimum(z, other), jnp.maximum(z, other)
        talks = high == low + 1
        if not relayed:
            talks = (low != high) & (talks | (high <= pivot) | (low >= pivot))
        count = count + talks.astype(jnp.int32)

        @pl.when(talks)
        def _():
            pl.semaphore_signal(barrier, inc=1, device_id={"ctx": other}, device_id_type=MESH)

    local_k, local_q = [], []
    for h in range(heads):
        part = pl.ds(h * HD, HD)
        local_k.append(pltpu.make_async_copy(k_hbm.at[:, part], kbuf.at[own, h], ksem.at[h]))
        local_q.append(pltpu.make_async_copy(q_hbm.at[:, part], qbuf.at[h, pl.ds(0, rows)], qsem.at[h]))
    for c in local_k[:2] + local_q[:2]:
        c.start()
    local_x = pltpu.make_async_copy(x_hbm, xb, xsem)
    local_x.start()
    small = [pltpu.make_async_copy(a, b, psem.at[i]) for i, (a, b) in enumerate(
        ((sf_hbm, sf_ref), (lf_hbm, lf_ref), (skip_hbm, skip_ref)))]
    for c in small:
        c.start()
    for c in local_k[2:] + local_q[2:]:
        c.start()

    local_x.wait()
    for j in range(3):
        rim_out[2 * j:2 * j + 2, :] = xb[j, rows - 2:rows, :]

    @pl.when(z == 0)
    def _():
        gprev[...] = jnp.zeros_like(gprev)

    pl.semaphore_wait(barrier, count)
    if relayed:
        inner = (z > 0) & (z < n - 1)
        for step in (-1, 1):
            @pl.when(inner)
            def _():
                pl.semaphore_signal(
                    ready, inc=1, device_id={"ctx": jnp.clip(z + step, 0, n - 1)}, device_id_type=MESH)

    up = jnp.minimum(z + 1, n - 1)
    rim = remote(rim_out, rim_in, rim_s, rim_r, "ctx", up)

    def gate(h):
        return remote(gown.at[h], gprev.at[h], gate_s.at[h], gate_r.at[h], "ctx", up)

    @pl.when(z < n - 1)
    def _():
        rim.start()

    def each_query(h, act, least=1, most=None):
        for other in range(pivot, n - 1):
            @pl.when((other + least <= z) & (z <= other + (most or n)))
            def _():
                act(remote(
                    qbuf.at[h, pl.ds(0, rows)],
                    qbuf.at[h, pl.ds(pl.multiple_of((z - other) * rows, rows), rows)],
                    q_s.at[other - pivot, h], q_r.at[z - other, h], "ctx", other))

    def each_key(h, act):
        for other in range(1, pivot + 1):
            @pl.when((other > z) & (z < pivot))
            def _():
                act(remote(kbuf.at[own, h], kbuf.at[own, h], k_s.at[other, h], k_r.at[own, h], "ctx", other))

    def each_value(h, act):
        for other in range(1, pivot + 1):
            @pl.when((other > z) & (z < pivot))
            def _():
                act(remote(vbuf.at[own, h], vbuf.at[own, h], v_s.at[other, h], v_r.at[own, h], "ctx", other))

    early = min(2, heads)
    steady = max(early, heads - 2)
    for h in range(early):
        local_k[h].wait()
        local_q[h].wait()
        each_key(h, lambda c: c.start())
        each_query(h, lambda c: c.start(), 1, 1)

    for c in small:
        c.wait()

    def featured(h, size, edge):
        part = pl.ds(pl.multiple_of(h * HD, HD), HD)
        row = lax.broadcasted_iota(jnp.int32, (size, HD), 0)
        feats = []
        for j in range(3):
            x = xb[j, 0:size, part].astype(F32)
            last = edge[2 * j + 1:2 * j + 2] if edge is not None else 0.0
            prior = edge[2 * j:2 * j + 1] if edge is not None else 0.0
            x1 = jnp.where(row == 0, last, pltpu.roll(x, 1, 0))
            x2 = jnp.where(row == 0, prior, jnp.where(row == 1, last, pltpu.roll(x, 2, 0)))
            total = sf_ref[0, j:j + 1, part].astype(F32) * x
            total = total + sf_ref[1, j:j + 1, part].astype(F32) * x1
            feats.append(total + sf_ref[2, j:j + 1, part].astype(F32) * x2)
        f0[h, 0:size] = feats[0]
        gown[h, 0:size] = (feats[1] * feats[2]).astype(BF)

    @pl.loop(0, heads)
    def _(h):
        featured(h, rows, None)

        @pl.when((z == 0) & (h < early))
        def _():
            gate(h).start()

    for c in local_k[early:] + local_q[early:]:
        c.wait()

    if relayed:
        pl.semaphore_wait(ready, (z > 1).astype(jnp.int32) + (z < n - 2).astype(jnp.int32))

    @pl.loop(0, heads)
    def _(h):
        each_query(h, lambda c: c.start(), 2)

        @pl.when(h >= early)
        def _():
            each_query(h, lambda c: c.start(), 1, 1)

    @pl.when(z > 0)
    def _():
        rim.wait_recv()

    @pl.loop(0, heads)
    def _(h):
        @pl.when(z > 0)
        def _():
            featured(h, 16, rim_in[:, pl.ds(pl.multiple_of(h * HD, HD), HD)].astype(F32))

        @pl.when((z > 0) & (z < n - 1) & ((z >= pivot) | (h < early)))
        def _():
            gate(h).start()

    half = heads // 2
    local_w, over_core = [], []
    for g in range(2):
        for d in range(chips):
            def columns(side):
                return w_hbm.at[pl.ds(g * half, half), :, pl.ds(pl.multiple_of(there(d, side) * cols, cols), cols)]

            def place(lo):
                return wv.at[pl.ds(g * half, half), pl.ds(lo, HD), pl.ds(d * cols, cols)]
            local_w.append(pltpu.make_async_copy(columns(core), place(0), wsem.at[g, d]))
            over_core.append(remote(columns(1 - core), place(HD), pw_s.at[g, d], pw_r.at[g, d], "mp", partner))
    for a, b in zip(local_w, over_core):
        a.start()
        b.start()

    slab = late // parts
    bit = HD // 2
    chunks = [(d, side, e, i) for d, side in beyond for e in range(slab) for i in range(2)]

    def late_part(src, owner, e, i):
        return wl.at[src, owner * slab + e, pl.ds(i * bit, bit)]

    def over_x(src, b, e, i):
        return remote(
            w_hbm.at[sure + part_at * slab + e, pl.ds(i * bit, bit), pl.ds(pl.multiple_of(b * cols, cols), cols)],
            late_part(src, part_at, e, i), wx_s.at[b, e, i], wx_r.at[src, e, i], "mp", b)

    def over_y(src, owner, e, i, d):
        ref = late_part(src, owner, e, i)
        return remote(ref, ref, wy_s.at[d, src, e, i], wy_r.at[owner, src, e, i],
                      "parts", lax.rem(part_at + d, parts))

    for d, side, e, i in chunks:
        over_x(me, at_side(d, side), e, i).start()

    def swap(d, side, e, i):
        src = at_side(d, side)
        over_x(src, src, e, i).wait_recv()
        for k in range(1, parts):
            over_y(src, part_at, e, i, k).start()

    flip = (lax.broadcasted_iota(jnp.int32, (tap_count, 2 * rows), 0)
            + lax.broadcasted_iota(jnp.int32, (tap_count, 2 * rows), 1)) == rows
    based = dot(lf_ref[...], flip.astype(BF))
    for g in range(groups):
        wide = jnp.broadcast_to(based[g:g + 1], (rows, 2 * rows))
        taps[g] = pltpu.roll(wide, 0, 1, stride=1, stride_axis=0).astype(BF)
    acc[...] = jnp.zeros_like(acc)

    lane = lax.broadcasted_iota(jnp.int32, (rows, HD), 1) // width

    def mix(h):
        @pl.when(z > 0)
        def _():
            gate(h).wait_recv()

        mine = gown[h]
        both = jnp.concatenate([gprev[h], mine], axis=0)
        filt = jnp.zeros((rows, HD), F32)
        for g in range(per_tile):
            filt = jnp.where(lane == g, dot(taps[h * per_tile + g], both), filt)
        part = pl.ds(pl.multiple_of(h * HD, HD), HD)
        val = f0[h] * (filt + skip_ref[:, part] * mine.astype(F32))
        vbuf[own, h] = val.T.astype(BF)

    def key_and_gate(h):
        each_key(h, lambda c: c.start())

        @pl.when(z < n - 1)
        def _():
            gate(h).start()

    @pl.when(z < pivot)
    def _():
        @pl.loop(0, heads)
        def _(h):
            @pl.when(h >= steady)
            def _():
                key_and_gate(h)

            mix(h)
            each_value(h, lambda c: c.start())

            @pl.when(h + early < steady)
            def _():
                key_and_gate(h + early)

    scale = HD ** -0.5
    krow = lax.broadcasted_iota(jnp.int32, (rows, span), 0)
    kcol = lax.broadcasted_iota(jnp.int32, (rows, span), 1)

    def each_part(h, act):
        for s in range(1, slots):
            @pl.when((z >= pivot) & (z + s < n))
            def _():
                act(s,
                    remote(sbuf.at[s - 1, h], pbuf.at[z - pivot, h],
                           o_s.at[s - 1, h], o_r.at[z - pivot, h], "ctx", z + s),
                    remote(sstat.at[s - 1, h], pstat.at[z - pivot, h],
                           t_s.at[s - 1, h], t_r.at[z - pivot, h], "ctx", z + s))

    def hand_over(h):
        def act(s, o, t):
            gi, at = (s * rows) // span, (s * rows) % span
            mm = mst[h, gi, :, at:at + rows]
            ll = lst[h, gi, :, at:at + rows]
            aa = ast[h, gi, :, at:at + rows]
            sbuf[s - 1, h] = (aa * (1.0 / ll[0:1])).astype(BF)
            sstat[s - 1, h] = mm[0:1] + jnp.log(ll[0:1])
            o.start()
            t.start()
        each_part(h, act)

    def queries_in(h):
        for s in range(1, slots):
            @pl.when((z >= pivot) & (z + s < n))
            def _():
                remote(qbuf.at[h, pl.ds(0, rows)], qbuf.at[h, pl.ds(s * rows, rows)],
                       q_s.at[0, h], q_r.at[s, h], "ctx", jnp.minimum(z + s, n - 1)).wait_recv()

    def own_keys(h):
        queries_in(h)
        for gi in range(query_groups):
            q = qbuf[h, gi * span:(gi + 1) * span]
            s = dot(kbuf[own, h], q, 1, 1) * scale
            s = jnp.where(krow <= kcol + gi * span, s, NEG)
            mx = jnp.max(s, axis=0, keepdims=True)
            p = jnp.exp(s - mx)
            mst[h, gi] = jnp.broadcast_to(mx, (8, span))
            lst[h, gi] = jnp.broadcast_to(jnp.sum(p, axis=0, keepdims=True), (8, span))
            ast[h, gi] = dot(vbuf[own, h], p.astype(BF))

    def key_in(j, h):
        return remote(kbuf.at[j, h], kbuf.at[j, h], k_s.at[0, 0], k_r.at[j, h], "ctx", j)

    def value_in(j, h):
        return remote(vbuf.at[j, h], vbuf.at[j, h], v_s.at[0, 0], v_r.at[j, h], "ctx", j)

    @pl.when(z > pivot)
    def _():
        @pl.loop(0, heads)
        def _(h):
            mix(h)
            own_keys(h)
            hand_over(h)

    def finished(h):
        att[h] = (ast[h, 0, :, 0:rows] * (1.0 / lst[h, 0, 0:1, 0:rows])).T.astype(BF)

    def front(h):
        s = dot(kbuf[0, h], qbuf[h, 0:rows], 1, 1) * scale
        s = jnp.where(krow[:, 0:rows] <= kcol[:, 0:rows], s, NEG)
        p = jnp.exp(s - jnp.max(s, axis=0, keepdims=True))
        o = dot(vbuf[0, h], p.astype(BF)) * (1.0 / jnp.sum(p, axis=0, keepdims=True))
        att[h] = o.T.astype(BF)

    def hub(h):
        key_in(0, h).wait_recv()
        queries_in(h)
        s = dot(jnp.concatenate([kbuf[0, h], kbuf[1, h]], axis=0), qbuf[h], 1, 1) * scale
        krow2 = lax.broadcasted_iota(jnp.int32, (2 * rows, span), 0) - rows
        kcol2 = lax.broadcasted_iota(jnp.int32, (2 * rows, span), 1)
        s = jnp.where(krow2 <= kcol2, s, NEG)
        mx = jnp.max(s, axis=0, keepdims=True)
        p = jnp.exp(s - mx)
        total = jnp.sum(p, axis=0, keepdims=True)
        p = p.astype(BF)
        inv = 1.0 / total
        lse = mx + jnp.log(total)
        mix(h)
        value_in(0, h).wait_recv()
        o = dot(jnp.concatenate([vbuf[0, h], vbuf[1, h]], axis=1), p) * inv

        def act(s, c, t):
            at = slice(s * rows, (s + 1) * rows)
            sbuf[s - 1, h] = o[:, at].astype(BF)
            sstat[s - 1, h] = lse[:, at]
            c.start()
            t.start()
        each_part(h, act)
        att[h] = o[:, 0:rows].T.astype(BF)

    def rear(h):
        @pl.loop(0, jnp.maximum(z - pivot, 0))
        def _(turn):
            j = z - pivot - 1 - turn
            remote(sbuf.at[0, 0], pbuf.at[j, h], o_s.at[0, 0], o_r.at[j, h], "ctx", j + pivot).wait_recv()
            remote(sstat.at[0, 0], pstat.at[j, h], t_s.at[0, 0], t_r.at[j, h], "ctx", j + pivot).wait_recv()
            old = mst[h, 0, :, 0:rows]
            lse = pstat[j, h]
            mx = jnp.maximum(old, lse)
            fade, gain = jnp.exp(old - mx), jnp.exp(lse - mx)
            mst[h, 0, :, 0:rows] = mx
            lst[h, 0, :, 0:rows] = lst[h, 0, :, 0:rows] * fade + gain
            ast[h, 0, :, 0:rows] = ast[h, 0, :, 0:rows] * fade[0:1] + pbuf[j, h].astype(F32) * gain[0:1]
        finished(h)

    def one_head(h):
        if joint:
            @pl.when(z < pivot)
            def _():
                front(h)

            @pl.when(z == pivot)
            def _():
                hub(h)
        else:
            @pl.when(z <= pivot)
            def _():
                @pl.when(z == pivot)
                def _():
                    mix(h)

                own_keys(h)

                @pl.loop(0, z)
                def _(j):
                    key_in(j, h).wait_recv()
                    value_in(j, h).wait_recv()
                    for gi in range(query_groups):
                        q = qbuf[h, gi * span:(gi + 1) * span]
                        s = dot(kbuf[j, h], q, 1, 1) * scale
                        old = mst[h, gi, 0:1]
                        mx = jnp.maximum(old, jnp.max(s, axis=0, keepdims=True))
                        p = jnp.exp(s - mx)
                        fade = jnp.exp(old - mx)
                        mst[h, gi] = jnp.broadcast_to(mx, (8, span))
                        lst[h, gi] = jnp.broadcast_to(
                            lst[h, gi, 0:1] * fade + jnp.sum(p, axis=0, keepdims=True), (8, span))
                        ast[h, gi] = ast[h, gi] * fade + dot(vbuf[j, h], p.astype(BF))

                @pl.when(z == pivot)
                def _():
                    hand_over(h)

                finished(h)

        @pl.when(z > pivot)
        def _():
            rear(h)

    def beside(h):
        return remote(att.at[h], pat.at[h], pat_s.at[h], pat_r.at[h], "mp", partner)

    def gathered(src, l, b):
        return remote(att.at[sure + l], atl.at[src, l], at_s.at[b, l], at_r.at[src, l], "mp", b)

    pieces = 4
    piece = cols // pieces

    def along(d, i):
        return remote(s2.at[d, i], r2.at[d, i], b_s.at[d, i], b_r.at[d, i], "mp", there(d, core))

    def weights_in(g):
        for d in range(chips):
            local_w[g * chips + d].wait()
            over_core[g * chips + d].wait_recv()

    def both_cores(h):
        beside(h).wait_recv()
        return jnp.concatenate([att[h], pat[h]], axis=1)

    def project(h, blocks):
        lhs = both_cores(h)
        for d in range(blocks):
            acc[d] += dot(lhs, wv[h, :, d * cols:(d + 1) * cols])

    @pl.loop(0, sure)
    def _(h):
        one_head(h)
        beside(h).start()

        @pl.when(h == 1)
        def _():
            weights_in(0)

        @pl.when(h == half)
        def _():
            weights_in(1)

        @pl.when(h > 0)
        def _():
            project(h - 1, chips)

        for k, chunk in enumerate(chunks):
            @pl.when(h == min(sure - 1, 1 + k * (sure - 1) // len(chunks)))
            def _():
                swap(*chunk)

    if half >= sure:
        weights_in(1)
    if sure < 2:
        weights_in(0)
    lhs = both_cores(sure - 1)
    for d in range(1, chips):
        for i in range(pieces):
            at = slice(i * piece, (i + 1) * piece)
            s2[d, i] = (acc[d, :, at] + dot(
                lhs, wv[sure - 1, :, d * cols + i * piece:d * cols + (i + 1) * piece])).astype(BF)
            along(d, i).start()
    acc[0] += dot(lhs, wv[sure - 1, :, 0:cols])

    @pl.loop(0, late)
    def _(l):
        one_head(sure + l)
        for d, side in beyond:
            gathered(me, l, at_side(d, side)).start()
        beside(sure + l).start()

        @pl.when(l > 0)
        def _():
            project(sure + l - 1, 1)

    if late:
        project(heads - 1, 1)
    for c in over_core:
        c.wait_send()
    for d, side, e, i in chunks:
        src = at_side(d, side)
        over_x(me, src, e, i).wait_send()
        for k in range(1, parts):
            over_y(src, part_at, e, i, k).wait_send()
    for l in range(late):
        for d, side in beyond:
            gathered(me, l, at_side(d, side)).wait_send()

    @pl.when(z < n - 1)
    def _():
        rim.wait_send()

    @pl.loop(0, heads)
    def _(h):
        def ended(s, o, t):
            o.wait_send()
            t.wait_send()
        beside(h).wait_send()

        @pl.when(z < n - 1)
        def _():
            gate(h).wait_send()

        each_query(h, lambda c: c.wait_send())
        each_key(h, lambda c: c.wait_send())
        each_value(h, lambda c: c.wait_send())
        each_part(h, ended)

    for d, side, e, i in chunks:
        for k in range(1, parts):
            owner = lax.rem(part_at + parts - k, parts)
            over_y(at_side(d, side), owner, e, i, k).wait_recv()
    if late:
        for d, side in beyond:
            src = at_side(d, side)
            for l in range(late):
                gathered(src, l, src).wait_recv()
    for i in range(pieces):
        at = slice(i * piece, (i + 1) * piece)
        total = acc[0, :, at]
        if late:
            for d, side in beyond:
                src = at_side(d, side)
                lhs = jnp.concatenate([atl[src, l] for l in range(late)], axis=1)
                total = total + dot(lhs, wl[src, :, :, at].reshape(late * HD, piece))
        for d in range(1, chips):
            along(d, i).wait_recv()
            total = total + r2[d, i].astype(F32)
        out_ref[:, at] = total.astype(BF)

    for i in range(pieces):
        for d in range(1, chips):
            along(d, i).wait_send()


def per_device(n, m, parts_n, inputs, short_filter, long_filter, skip_gain, queries, key_rows, out_weight):
    rows, _, channels = inputs.shape
    heads = channels // HD
    groups = long_filter.shape[0]
    total = out_weight.shape[1]
    cols = total // m
    chips = m // 2
    pivot = n // 3
    slots = n - pivot
    batch = min(3, slots)
    padded = -(-slots // batch) * batch
    span = batch * rows
    gq = padded // batch
    parts = max(slots - 1, 1)
    late = LATE if LATE % parts_n == 0 and heads > LATE + 1 else 0
    slab = max(late // parts_n, 1)
    vm = pltpu.VMEM
    dma = pltpu.SemaphoreType.DMA
    scratch = [
        vm(short_filter.shape, BF), vm(long_filter.shape, BF), vm((1, channels), F32), dma((3,)),
        vm((3, rows, channels), BF), vm((16, channels), BF), vm((16, channels), BF),
        vm((heads, rows, HD), F32), vm((heads, rows, HD), BF), vm((heads, rows, HD), BF),
        vm((groups, rows, 2 * rows), BF),
        vm((pivot + 1, heads, rows, HD), BF), vm((pivot + 1, heads, HD, rows), BF),
        vm((heads, padded * rows, HD), BF),
        vm((heads, gq, 8, span), F32), vm((heads, gq, 8, span), F32), vm((heads, gq, HD, span), F32),
        vm((parts, heads, HD, rows), BF), vm((parts, heads, 1, rows), F32),
        vm((parts, heads, HD, rows), BF), vm((parts, heads, 1, rows), F32),
        vm((heads, rows, HD), BF), vm((heads, rows, HD), BF),
        vm((heads, 2 * HD, chips * cols), BF), vm((chips, rows, cols), F32),
        vm((chips, 4, rows, cols // 4), BF), vm((chips, 4, rows, cols // 4), BF),
        vm((m, max(late, 1), HD, cols), BF), vm((m, max(late, 1), rows, HD), BF),
        dma, dma((heads,)), dma((heads,)), dma((2, chips)), dma, dma, dma((heads,)), dma((heads,)),
    ] + [dma((pivot + 1, heads))] * 4 + [dma((slots, heads))] * 2 + [
        dma((parts, heads)), dma((parts, heads)), dma((parts, heads)), dma((parts, heads)),
    ] + [dma((chips, 4))] * 2 + [pltpu.SemaphoreType.REGULAR] + [
        dma((2, chips)), dma((2, chips)), dma((heads,)), dma((heads,)),
        dma((m, slab, 2)), dma((m, slab, 2)), dma((parts_n, m, slab, 2)), dma((parts_n, m, slab, 2)),
        dma((m, max(late, 1))), dma((m, max(late, 1))),
    ]
    in_vmem = pl.BlockSpec(memory_space=pltpu.VMEM)
    in_hbm = pl.BlockSpec(memory_space=pl.ANY)
    return pl.pallas_call(
        functools.partial(kernel, n, m, parts_n, late),
        out_shape=pltpu.VMEM((rows, cols), BF),
        in_specs=[in_hbm] * 7,
        out_specs=in_vmem,
        scratch_shapes=scratch,
        compiler_params=pltpu.CompilerParams(
            collective_id=0, has_side_effects=True, vmem_limit_bytes=60 * 2**20),
    )(inputs.transpose(1, 0, 2), short_filter, long_filter, skip_gain[None], queries, key_rows,
      out_weight.reshape(heads, HD, total))


def solution(mesh):
    placed = (
        P(("parts", "ctx"), None, "mp"),
        P(None, None, "mp"),
        P("mp", None),
        P("mp"),
        P(("parts", "ctx"), "mp"),
        P(("parts", "ctx"), "mp"),
        P("mp", None),
    )
    return jax.shard_map(
        functools.partial(per_device, mesh.shape["ctx"], mesh.shape["mp"], mesh.shape["parts"]),
        mesh=mesh, in_specs=placed, out_specs=P(("parts", "ctx"), "mp"), check_vma=False)
```

```python
import functools

import jax
import jax.numpy as jnp
from jax import lax
from jax.experimental import pallas as pl
from jax.experimental.pallas import tpu as pltpu
from jax.sharding import PartitionSpec as P

HD = 128
LATE = 0
MESH = pl.DeviceIdType.MESH
NEG = -1e30
F32 = jnp.float32
BF = jnp.bfloat16


def dot(a, b, ca=1, cb=0):
    return lax.dot_general(a, b, (((ca,), (cb,)), ((), ())), preferred_element_type=F32)


def kernel(
    n, m, parts, late, x_hbm, sf_hbm, lf_hbm, skip_hbm, q_hbm, k_hbm, w_hbm, out_ref,
    sf_ref, lf_ref, skip_ref, psem, xb, rim_out, rim_in, f0, gown, gprev, taps, kbuf, vbuf, qbuf, mst, lst, ast,
    sbuf, sstat, pbuf, pstat, att, pat, wv, acc, s2, r2, wl, atl,
    xsem, qsem, ksem, wsem, rim_s, rim_r, gate_s, gate_r, k_s, k_r, v_s, v_r,
    q_s, q_r, o_s, o_r, t_s, t_r, b_s, b_r, ready,
    pw_s, pw_r, pat_s, pat_r, wx_s, wx_r, wy_s, wy_r, at_s, at_r,
):
    z = lax.axis_index("ctx")
    me = lax.axis_index("mp")
    part_at = lax.axis_index("parts")
    core = lax.rem(me, 2)
    chip = me // 2
    chips = m // 2
    partner = chip * 2 + 1 - core
    pivot = n // 3
    slots = n - pivot
    rows = xb.shape[1]
    heads = gown.shape[0]
    groups = lf_ref.shape[0]
    per_tile = groups // heads
    width = HD // per_tile
    tap_count = lf_ref.shape[1]
    span = min(3, slots) * rows
    query_groups = qbuf.shape[1] // span
    cols = out_ref.shape[1]
    own = jnp.minimum(z, pivot)
    sure = heads - late
    joint = pivot == 1 and query_groups == 1

    def remote(src, dst, ss, rs, axis, target):
        return pltpu.make_async_remote_copy(
            src_ref=src, dst_ref=dst, send_sem=ss, recv_sem=rs,
            device_id={axis: target}, device_id_type=MESH)

    def there(d, side):
        return lax.rem(chip + d, chips) * 2 + side

    beyond = [(d, side) for d in range(1, chips) for side in range(2)]

    def at_side(d, side):
        return there(d, jnp.abs(core - side))

    barrier = pltpu.get_barrier_semaphore()
    hops = max(pivot, n - 1 - pivot)
    relayed = hops == 2
    pl.semaphore_signal(barrier, inc=1, device_id={"mp": partner}, device_id_type=MESH)
    for d, side in beyond:
        if late or side == 0:
            pl.semaphore_signal(barrier, inc=1, device_id={"mp": at_side(d, side)}, device_id_type=MESH)
    for d in range(1, parts):
        if late:
            pl.semaphore_signal(
                barrier, inc=1, device_id={"parts": lax.rem(part_at + d, parts)}, device_id_type=MESH)
    count = jnp.int32(m - 1 + parts - 1 if late else chips)
    for other in range(n):
        low, high = jnp.minimum(z, other), jnp.maximum(z, other)
        talks = high == low + 1
        if not relayed:
            talks = (low != high) & (talks | (high <= pivot) | (low >= pivot))
        count = count + talks.astype(jnp.int32)

        @pl.when(talks)
        def _():
            pl.semaphore_signal(barrier, inc=1, device_id={"ctx": other}, device_id_type=MESH)

    local_k, local_q = [], []
    for h in range(heads):
        part = pl.ds(h * HD, HD)
        local_k.append(pltpu.make_async_copy(k_hbm.at[:, part], kbuf.at[own, h], ksem.at[h]))
        local_q.append(pltpu.make_async_copy(q_hbm.at[:, part], qbuf.at[h, pl.ds(0, rows)], qsem.at[h]))
    for c in local_k[:2] + local_q[:2]:
        c.start()
    local_x = pltpu.make_async_copy(x_hbm, xb, xsem)
    local_x.start()
    small = [pltpu.make_async_copy(a, b, psem.at[i]) for i, (a, b) in enumerate(
        ((sf_hbm, sf_ref), (lf_hbm, lf_ref), (skip_hbm, skip_ref)))]
    for c in small:
        c.start()
    for c in local_k[2:] + local_q[2:]:
        c.start()

    local_x.wait()
    wing = rim_out.shape[1]
    for j in range(3):
        for g in range(2):
            rim_out[8 * g + 2 * j:8 * g + 2 * j + 2, :] = xb[j, rows - 2:rows, g * wing:(g + 1) * wing]

    @pl.when(z == 0)
    def _():
        gprev[...] = jnp.zeros_like(gprev)

    pl.semaphore_wait(barrier, count)
    if relayed:
        inner = (z > 0) & (z < n - 1)
        for step in (-1, 1):
            @pl.when(inner)
            def _():
                pl.semaphore_signal(
                    ready, inc=1, device_id={"ctx": jnp.clip(z + step, 0, n - 1)}, device_id_type=MESH)

    up = jnp.minimum(z + 1, n - 1)
    rim = remote(rim_out, rim_in, rim_s, rim_r, "ctx", up)

    def gate(h):
        return remote(gown.at[h], gprev.at[h], gate_s.at[h], gate_r.at[h], "ctx", up)

    @pl.when(z < n - 1)
    def _():
        rim.start()

    def each_query(h, act, least=1, most=None):
        for other in range(pivot, n - 1):
            @pl.when((other + least <= z) & (z <= other + (most or n)))
            def _():
                act(remote(
                    qbuf.at[h, pl.ds(0, rows)],
                    qbuf.at[h, pl.ds(pl.multiple_of((z - other) * rows, rows), rows)],
                    q_s.at[other - pivot, h], q_r.at[z - other, h], "ctx", other))

    def each_key(h, act):
        for other in range(1, pivot + 1):
            @pl.when((other > z) & (z < pivot))
            def _():
                act(remote(kbuf.at[own, h], kbuf.at[own, h], k_s.at[other, h], k_r.at[own, h], "ctx", other))

    def each_value(h, act):
        for other in range(1, pivot + 1):
            @pl.when((other > z) & (z < pivot))
            def _():
                act(remote(vbuf.at[own, h], vbuf.at[own, h], v_s.at[other, h], v_r.at[own, h], "ctx", other))

    early = min(2, heads)
    steady = max(early, heads - 2)
    for h in range(early):
        local_k[h].wait()
        local_q[h].wait()
        each_key(h, lambda c: c.start())
        each_query(h, lambda c: c.start(), 1, 1)

    for c in small:
        c.wait()

    def featured(h, size, edge):
        part = pl.ds(pl.multiple_of(h * HD, HD), HD)
        row = lax.broadcasted_iota(jnp.int32, (size, HD), 0)
        feats = []
        for j in range(3):
            x = xb[j, 0:size, part].astype(F32)
            last = edge[2 * j + 1:2 * j + 2] if edge is not None else 0.0
            prior = edge[2 * j:2 * j + 1] if edge is not None else 0.0
            x1 = jnp.where(row == 0, last, pltpu.roll(x, 1, 0))
            x2 = jnp.where(row == 0, prior, jnp.where(row == 1, last, pltpu.roll(x, 2, 0)))
            total = sf_ref[0, j:j + 1, part].astype(F32) * x
            total = total + sf_ref[1, j:j + 1, part].astype(F32) * x1
            feats.append(total + sf_ref[2, j:j + 1, part].astype(F32) * x2)
        f0[h, 0:size] = feats[0]
        gown[h, 0:size] = (feats[1] * feats[2]).astype(BF)

    @pl.loop(0, heads)
    def _(h):
        featured(h, rows, None)

        @pl.when((z == 0) & (h < early))
        def _():
            gate(h).start()

    for c in local_k[early:] + local_q[early:]:
        c.wait()

    if relayed:
        pl.semaphore_wait(ready, (z > 1).astype(jnp.int32) + (z < n - 2).astype(jnp.int32))

    @pl.loop(0, heads)
    def _(h):
        each_query(h, lambda c: c.start(), 2)

        @pl.when(h >= early)
        def _():
            each_query(h, lambda c: c.start(), 1, 1)

    @pl.when(z > 0)
    def _():
        rim.wait_recv()

    @pl.loop(0, heads)
    def _(h):
        @pl.when(z > 0)
        def _():
            both = rim_in[:, pl.ds(pl.multiple_of(lax.rem(h * HD, wing), HD), HD)].astype(F32)
            featured(h, 16, jnp.where(h * HD < wing, both[0:8], both[8:16]))

        @pl.when((z > 0) & (z < n - 1) & ((z >= pivot) | (h < early)))
        def _():
            gate(h).start()

    half = heads // 2
    local_w, over_core = [], []
    for g in range(2):
        for d in range(chips):
            def columns(side):
                return w_hbm.at[pl.ds(g * half, half), :, pl.ds(pl.multiple_of(there(d, side) * cols, cols), cols)]

            def place(lo):
                return wv.at[pl.ds(g * half, half), pl.ds(lo, HD), pl.ds(d * cols, cols)]
            local_w.append(pltpu.make_async_copy(columns(core), place(0), wsem.at[g, d]))
            over_core.append(remote(columns(1 - core), place(HD), pw_s.at[g, d], pw_r.at[g, d], "mp", partner))

    slab = late // parts
    bit = HD // 2
    chunks = [(d, side, e, i) for d, side in beyond for e in range(slab) for i in range(2)]

    def late_part(src, owner, e, i):
        return wl.at[src, owner * slab + e, pl.ds(i * bit, bit)]

    def over_x(src, b, e, i):
        return remote(
            w_hbm.at[sure + part_at * slab + e, pl.ds(i * bit, bit), pl.ds(pl.multiple_of(b * cols, cols), cols)],
            late_part(src, part_at, e, i), wx_s.at[b, e, i], wx_r.at[src, e, i], "mp", b)

    def over_y(src, owner, e, i, d):
        ref = late_part(src, owner, e, i)
        return remote(ref, ref, wy_s.at[d, src, e, i], wy_r.at[owner, src, e, i],
                      "parts", lax.rem(part_at + d, parts))

    for d, side, e, i in chunks:
        over_x(me, at_side(d, side), e, i).start()

    def swap(d, side, e, i):
        src = at_side(d, side)
        over_x(src, src, e, i).wait_recv()
        for k in range(1, parts):
            over_y(src, part_at, e, i, k).start()

    flip = (lax.broadcasted_iota(jnp.int32, (tap_count, 2 * rows), 0)
            + lax.broadcasted_iota(jnp.int32, (tap_count, 2 * rows), 1)) == rows
    based = dot(lf_ref[...], flip.astype(BF))
    for g in range(groups):
        wide = jnp.broadcast_to(based[g:g + 1], (rows, 2 * rows))
        taps[g] = pltpu.roll(wide, 0, 1, stride=1, stride_axis=0).astype(BF)
    acc[...] = jnp.zeros_like(acc)

    lane = lax.broadcasted_iota(jnp.int32, (rows, HD), 1) // width

    def mix(h):
        @pl.when(z > 0)
        def _():
            gate(h).wait_recv()

        mine = gown[h]
        both = jnp.concatenate([gprev[h], mine], axis=0)
        filt = jnp.zeros((rows, HD), F32)
        for g in range(per_tile):
            filt = jnp.where(lane == g, dot(taps[h * per_tile + g], both), filt)
        part = pl.ds(pl.multiple_of(h * HD, HD), HD)
        val = f0[h] * (filt + skip_ref[:, part] * mine.astype(F32))
        vbuf[own, h] = val.T.astype(BF)

    def key_and_gate(h):
        each_key(h, lambda c: c.start())

        @pl.when(z < n - 1)
        def _():
            gate(h).start()

    @pl.when(z < pivot)
    def _():
        @pl.loop(0, heads)
        def _(h):
            @pl.when(h >= steady)
            def _():
                key_and_gate(h)

            mix(h)
            each_value(h, lambda c: c.start())

            @pl.when(h + early < steady)
            def _():
                key_and_gate(h + early)

    for a, b in zip(local_w, over_core):
        a.start()
        b.start()

    scale = HD ** -0.5
    krow = lax.broadcasted_iota(jnp.int32, (rows, span), 0)
    kcol = lax.broadcasted_iota(jnp.int32, (rows, span), 1)

    def each_part(h, act):
        for s in range(1, slots):
            @pl.when((z >= pivot) & (z + s < n))
            def _():
                act(s,
                    remote(sbuf.at[s - 1, h], pbuf.at[z - pivot, h],
                           o_s.at[s - 1, h], o_r.at[z - pivot, h], "ctx", z + s),
                    remote(sstat.at[s - 1, h], pstat.at[z - pivot, h],
                           t_s.at[s - 1, h], t_r.at[z - pivot, h], "ctx", z + s))

    def hand_over(h):
        def act(s, o, t):
            gi, at = (s * rows) // span, (s * rows) % span
            mm = mst[h, gi, :, at:at + rows]
            ll = lst[h, gi, :, at:at + rows]
            aa = ast[h, gi, :, at:at + rows]
            sbuf[s - 1, h] = (aa * (1.0 / ll[0:1])).astype(BF)
            sstat[s - 1, h] = mm[0:1] + jnp.log(ll[0:1])
            o.start()
            t.start()
        each_part(h, act)

    def queries_in(h):
        for s in range(1, slots):
            @pl.when((z >= pivot) & (z + s < n))
            def _():
                remote(qbuf.at[h, pl.ds(0, rows)], qbuf.at[h, pl.ds(s * rows, rows)],
                       q_s.at[0, h], q_r.at[s, h], "ctx", jnp.minimum(z + s, n - 1)).wait_recv()

    def own_keys(h):
        queries_in(h)
        for gi in range(query_groups):
            q = qbuf[h, gi * span:(gi + 1) * span]
            s = dot(kbuf[own, h], q, 1, 1) * scale
            s = jnp.where(krow <= kcol + gi * span, s, NEG)
            mx = jnp.max(s, axis=0, keepdims=True)
            p = jnp.exp(s - mx)
            mst[h, gi] = jnp.broadcast_to(mx, (8, span))
            lst[h, gi] = jnp.broadcast_to(jnp.sum(p, axis=0, keepdims=True), (8, span))
            ast[h, gi] = dot(vbuf[own, h], p.astype(BF))

    def key_in(j, h):
        return remote(kbuf.at[j, h], kbuf.at[j, h], k_s.at[0, 0], k_r.at[j, h], "ctx", j)

    def value_in(j, h):
        return remote(vbuf.at[j, h], vbuf.at[j, h], v_s.at[0, 0], v_r.at[j, h], "ctx", j)

    @pl.when(z > pivot)
    def _():
        @pl.loop(0, heads)
        def _(h):
            mix(h)
            own_keys(h)
            hand_over(h)

    def finished(h):
        att[h] = (ast[h, 0, :, 0:rows] * (1.0 / lst[h, 0, 0:1, 0:rows])).T.astype(BF)

    def front(h):
        s = dot(kbuf[0, h], qbuf[h, 0:rows], 1, 1) * scale
        s = jnp.where(krow[:, 0:rows] <= kcol[:, 0:rows], s, NEG)
        p = jnp.exp(s - jnp.max(s, axis=0, keepdims=True))
        o = dot(vbuf[0, h], p.astype(BF)) * (1.0 / jnp.sum(p, axis=0, keepdims=True))
        att[h] = o.T.astype(BF)

    def hub(h):
        key_in(0, h).wait_recv()
        queries_in(h)
        s = dot(jnp.concatenate([kbuf[0, h], kbuf[1, h]], axis=0), qbuf[h], 1, 1) * scale
        krow2 = lax.broadcasted_iota(jnp.int32, (2 * rows, span), 0) - rows
        kcol2 = lax.broadcasted_iota(jnp.int32, (2 * rows, span), 1)
        s = jnp.where(krow2 <= kcol2, s, NEG)
        mx = jnp.max(s, axis=0, keepdims=True)
        p = jnp.exp(s - mx)
        total = jnp.sum(p, axis=0, keepdims=True)
        p = p.astype(BF)
        inv = 1.0 / total
        lse = mx + jnp.log(total)
        mix(h)
        value_in(0, h).wait_recv()
        o = dot(jnp.concatenate([vbuf[0, h], vbuf[1, h]], axis=1), p) * inv

        def act(s, c, t):
            at = slice(s * rows, (s + 1) * rows)
            sbuf[s - 1, h] = o[:, at].astype(BF)
            sstat[s - 1, h] = lse[:, at]
            c.start()
            t.start()
        each_part(h, act)
        att[h] = o[:, 0:rows].T.astype(BF)

    def rear(h):
        @pl.loop(0, jnp.maximum(z - pivot, 0))
        def _(turn):
            j = z - pivot - 1 - turn
            remote(sbuf.at[0, 0], pbuf.at[j, h], o_s.at[0, 0], o_r.at[j, h], "ctx", j + pivot).wait_recv()
            remote(sstat.at[0, 0], pstat.at[j, h], t_s.at[0, 0], t_r.at[j, h], "ctx", j + pivot).wait_recv()
            old = mst[h, 0, :, 0:rows]
            lse = pstat[j, h]
            mx = jnp.maximum(old, lse)
            fade, gain = jnp.exp(old - mx), jnp.exp(lse - mx)
            mst[h, 0, :, 0:rows] = mx
            lst[h, 0, :, 0:rows] = lst[h, 0, :, 0:rows] * fade + gain
            ast[h, 0, :, 0:rows] = ast[h, 0, :, 0:rows] * fade[0:1] + pbuf[j, h].astype(F32) * gain[0:1]
        finished(h)

    def one_head(h):
        if joint:
            @pl.when(z < pivot)
            def _():
                front(h)

            @pl.when(z == pivot)
            def _():
                hub(h)
        else:
            @pl.when(z <= pivot)
            def _():
                @pl.when(z == pivot)
                def _():
                    mix(h)

                own_keys(h)

                @pl.loop(0, z)
                def _(j):
                    key_in(j, h).wait_recv()
                    value_in(j, h).wait_recv()
                    for gi in range(query_groups):
                        q = qbuf[h, gi * span:(gi + 1) * span]
                        s = dot(kbuf[j, h], q, 1, 1) * scale
                        old = mst[h, gi, 0:1]
                        mx = jnp.maximum(old, jnp.max(s, axis=0, keepdims=True))
                        p = jnp.exp(s - mx)
                        fade = jnp.exp(old - mx)
                        mst[h, gi] = jnp.broadcast_to(mx, (8, span))
                        lst[h, gi] = jnp.broadcast_to(
                            lst[h, gi, 0:1] * fade + jnp.sum(p, axis=0, keepdims=True), (8, span))
                        ast[h, gi] = ast[h, gi] * fade + dot(vbuf[j, h], p.astype(BF))

                @pl.when(z == pivot)
                def _():
                    hand_over(h)

                finished(h)

        @pl.when(z > pivot)
        def _():
            rear(h)

    def beside(h):
        return remote(att.at[h], pat.at[h], pat_s.at[h], pat_r.at[h], "mp", partner)

    def gathered(src, l, b):
        return remote(att.at[sure + l], atl.at[src, l], at_s.at[b, l], at_r.at[src, l], "mp", b)

    pieces = 4
    piece = cols // pieces

    def along(d, i):
        return remote(s2.at[d, i], r2.at[d, i], b_s.at[d, i], b_r.at[d, i], "mp", there(d, core))

    def weights_in(g):
        for d in range(chips):
            local_w[g * chips + d].wait()
            over_core[g * chips + d].wait_recv()

    def both_cores(h):
        beside(h).wait_recv()
        return jnp.concatenate([att[h], pat[h]], axis=1)

    def project(h, blocks):
        lhs = both_cores(h)
        for d in range(blocks):
            acc[d] += dot(lhs, wv[h, :, d * cols:(d + 1) * cols])

    @pl.loop(0, sure)
    def _(h):
        one_head(h)
        beside(h).start()

        @pl.when(h == 1)
        def _():
            weights_in(0)

        @pl.when(h == half)
        def _():
            weights_in(1)

        @pl.when(h > 0)
        def _():
            project(h - 1, chips)

        for k, chunk in enumerate(chunks):
            @pl.when(h == min(sure - 1, 1 + k * (sure - 1) // len(chunks)))
            def _():
                swap(*chunk)

    if half >= sure:
        weights_in(1)
    if sure < 2:
        weights_in(0)
    lhs = both_cores(sure - 1)
    for d in range(1, chips):
        for i in range(pieces):
            at = slice(i * piece, (i + 1) * piece)
            s2[d, i] = (acc[d, :, at] + dot(
                lhs, wv[sure - 1, :, d * cols + i * piece:d * cols + (i + 1) * piece])).astype(BF)
            along(d, i).start()
    acc[0] += dot(lhs, wv[sure - 1, :, 0:cols])

    @pl.loop(0, late)
    def _(l):
        one_head(sure + l)
        for d, side in beyond:
            gathered(me, l, at_side(d, side)).start()
        beside(sure + l).start()

        @pl.when(l > 0)
        def _():
            project(sure + l - 1, 1)

    if late:
        project(heads - 1, 1)
    for c in over_core:
        c.wait_send()
    for d, side, e, i in chunks:
        src = at_side(d, side)
        over_x(me, src, e, i).wait_send()
        for k in range(1, parts):
            over_y(src, part_at, e, i, k).wait_send()
    for l in range(late):
        for d, side in beyond:
            gathered(me, l, at_side(d, side)).wait_send()

    @pl.when(z < n - 1)
    def _():
        rim.wait_send()

    @pl.loop(0, heads)
    def _(h):
        def ended(s, o, t):
            o.wait_send()
            t.wait_send()
        beside(h).wait_send()

        @pl.when(z < n - 1)
        def _():
            gate(h).wait_send()

        each_query(h, lambda c: c.wait_send())
        each_key(h, lambda c: c.wait_send())
        each_value(h, lambda c: c.wait_send())
        each_part(h, ended)

    for d, side, e, i in chunks:
        for k in range(1, parts):
            owner = lax.rem(part_at + parts - k, parts)
            over_y(at_side(d, side), owner, e, i, k).wait_recv()
    if late:
        for d, side in beyond:
            src = at_side(d, side)
            for l in range(late):
                gathered(src, l, src).wait_recv()
    for i in range(pieces):
        at = slice(i * piece, (i + 1) * piece)
        total = acc[0, :, at]
        if late:
            for d, side in beyond:
                src = at_side(d, side)
                lhs = jnp.concatenate([atl[src, l] for l in range(late)], axis=1)
                total = total + dot(lhs, wl[src, :, :, at].reshape(late * HD, piece))
        for d in range(1, chips):
            along(d, i).wait_recv()
            total = total + r2[d, i].astype(F32)
        out_ref[:, at] = total.astype(BF)

    for i in range(pieces):
        for d in range(1, chips):
            along(d, i).wait_send()


def per_device(n, m, parts_n, inputs, short_filter, long_filter, skip_gain, queries, key_rows, out_weight):
    rows, _, channels = inputs.shape
    heads = channels // HD
    groups = long_filter.shape[0]
    total = out_weight.shape[1]
    cols = total // m
    chips = m // 2
    pivot = n // 3
    slots = n - pivot
    batch = min(3, slots)
    padded = -(-slots // batch) * batch
    span = batch * rows
    gq = padded // batch
    parts = max(slots - 1, 1)
    late = LATE if LATE % parts_n == 0 and heads > LATE + 1 else 0
    slab = max(late // parts_n, 1)
    vm = pltpu.VMEM
    dma = pltpu.SemaphoreType.DMA
    scratch = [
        vm(short_filter.shape, BF), vm(long_filter.shape, BF), vm((1, channels), F32), dma((3,)),
        vm((3, rows, channels), BF), vm((16, channels // 2), BF), vm((16, channels // 2), BF),
        vm((heads, rows, HD), F32), vm((heads, rows, HD), BF), vm((heads, rows, HD), BF),
        vm((groups, rows, 2 * rows), BF),
        vm((pivot + 1, heads, rows, HD), BF), vm((pivot + 1, heads, HD, rows), BF),
        vm((heads, padded * rows, HD), BF),
        vm((heads, gq, 8, span), F32), vm((heads, gq, 8, span), F32), vm((heads, gq, HD, span), F32),
        vm((parts, heads, HD, rows), BF), vm((parts, heads, 1, rows), F32),
        vm((parts, heads, HD, rows), BF), vm((parts, heads, 1, rows), F32),
        vm((heads, rows, HD), BF), vm((heads, rows, HD), BF),
        vm((heads, 2 * HD, chips * cols), BF), vm((chips, rows, cols), F32),
        vm((chips, 4, rows, cols // 4), BF), vm((chips, 4, rows, cols // 4), BF),
        vm((m, max(late, 1), HD, cols), BF), vm((m, max(late, 1), rows, HD), BF),
        dma, dma((heads,)), dma((heads,)), dma((2, chips)), dma, dma, dma((heads,)), dma((heads,)),
    ] + [dma((pivot + 1, heads))] * 4 + [dma((slots, heads))] * 2 + [
        dma((parts, heads)), dma((parts, heads)), dma((parts, heads)), dma((parts, heads)),
    ] + [dma((chips, 4))] * 2 + [pltpu.SemaphoreType.REGULAR] + [
        dma((2, chips)), dma((2, chips)), dma((heads,)), dma((heads,)),
        dma((m, slab, 2)), dma((m, slab, 2)), dma((parts_n, m, slab, 2)), dma((parts_n, m, slab, 2)),
        dma((m, max(late, 1))), dma((m, max(late, 1))),
    ]
    in_vmem = pl.BlockSpec(memory_space=pltpu.VMEM)
    in_hbm = pl.BlockSpec(memory_space=pl.ANY)
    return pl.pallas_call(
        functools.partial(kernel, n, m, parts_n, late),
        out_shape=pltpu.VMEM((rows, cols), BF),
        in_specs=[in_hbm] * 7,
        out_specs=in_vmem,
        scratch_shapes=scratch,
        compiler_params=pltpu.CompilerParams(
            collective_id=0, has_side_effects=True, vmem_limit_bytes=60 * 2**20),
    )(inputs.transpose(1, 0, 2), short_filter, long_filter, skip_gain[None], queries, key_rows,
      out_weight.reshape(heads, HD, total))


def solution(mesh):
    placed = (
        P(("parts", "ctx"), None, "mp"),
        P(None, None, "mp"),
        P("mp", None),
        P("mp"),
        P(("parts", "ctx"), "mp"),
        P(("parts", "ctx"), "mp"),
        P("mp", None),
    )
    return jax.shard_map(
        functools.partial(per_device, mesh.shape["ctx"], mesh.shape["mp"], mesh.shape["parts"]),
        mesh=mesh, in_specs=placed, out_specs=P(("parts", "ctx"), "mp"), check_vma=False)
```

```python
import functools

import jax
import jax.numpy as jnp
from jax import lax
from jax.experimental import pallas as pl
from jax.experimental.pallas import tpu as pltpu
from jax.sharding import PartitionSpec as P

HD = 128
LATE = 0
MESH = pl.DeviceIdType.MESH
NEG = -1e30
F32 = jnp.float32
BF = jnp.bfloat16


def dot(a, b, ca=1, cb=0):
    return lax.dot_general(a, b, (((ca,), (cb,)), ((), ())), preferred_element_type=F32)


def kernel(
    n, m, parts, late, x_hbm, sf_hbm, lf_hbm, skip_hbm, q_hbm, k_hbm, w_hbm, out_ref,
    sf_ref, lf_ref, skip_ref, psem, xb, rim_out, rim_in, f0, gown, gprev, taps, kbuf, vbuf, qbuf, mst, lst, ast,
    sbuf, sstat, pbuf, pstat, att, pat, wv, acc, s2, r2, wl, atl,
    xsem, qsem, ksem, wsem, rim_s, rim_r, gate_s, gate_r, k_s, k_r, v_s, v_r,
    q_s, q_r, o_s, o_r, t_s, t_r, b_s, b_r, ready,
    pw_s, pw_r, pat_s, pat_r, wx_s, wx_r, wy_s, wy_r, at_s, at_r,
):
    z = lax.axis_index("ctx")
    me = lax.axis_index("mp")
    part_at = lax.axis_index("parts")
    core = lax.rem(me, 2)
    chip = me // 2
    chips = m // 2
    partner = chip * 2 + 1 - core
    pivot = n // 3
    slots = n - pivot
    rows = xb.shape[1]
    heads = gown.shape[0]
    groups = lf_ref.shape[0]
    per_tile = groups // heads
    width = HD // per_tile
    tap_count = lf_ref.shape[1]
    span = min(3, slots) * rows
    query_groups = qbuf.shape[1] // span
    cols = out_ref.shape[1]
    own = jnp.minimum(z, pivot)
    sure = heads - late
    joint = pivot == 1 and query_groups == 1

    def remote(src, dst, ss, rs, axis, target):
        return pltpu.make_async_remote_copy(
            src_ref=src, dst_ref=dst, send_sem=ss, recv_sem=rs,
            device_id={axis: target}, device_id_type=MESH)

    def there(d, side):
        return lax.rem(chip + d, chips) * 2 + side

    beyond = [(d, side) for d in range(1, chips) for side in range(2)]

    def at_side(d, side):
        return there(d, jnp.abs(core - side))

    barrier = pltpu.get_barrier_semaphore()
    hops = max(pivot, n - 1 - pivot)
    relayed = hops == 2
    pl.semaphore_signal(barrier, inc=1, device_id={"mp": partner}, device_id_type=MESH)
    for d, side in beyond:
        if late or side == 0:
            pl.semaphore_signal(barrier, inc=1, device_id={"mp": at_side(d, side)}, device_id_type=MESH)
    for d in range(1, parts):
        if late:
            pl.semaphore_signal(
                barrier, inc=1, device_id={"parts": lax.rem(part_at + d, parts)}, device_id_type=MESH)
    count = jnp.int32(m - 1 + parts - 1 if late else chips)
    for other in range(n):
        low, high = jnp.minimum(z, other), jnp.maximum(z, other)
        talks = high == low + 1
        if not relayed:
            talks = (low != high) & (talks | (high <= pivot) | (low >= pivot))
        count = count + talks.astype(jnp.int32)

        @pl.when(talks)
        def _():
            pl.semaphore_signal(barrier, inc=1, device_id={"ctx": other}, device_id_type=MESH)

    local_k, local_q = [], []
    for h in range(heads):
        part = pl.ds(h * HD, HD)
        local_k.append(pltpu.make_async_copy(k_hbm.at[:, part], kbuf.at[own, h], ksem.at[h]))
        local_q.append(pltpu.make_async_copy(q_hbm.at[:, part], qbuf.at[h, pl.ds(0, rows)], qsem.at[h]))
    for c in local_k[:2] + local_q[:2]:
        c.start()
    local_x = pltpu.make_async_copy(x_hbm, xb, xsem)
    local_x.start()
    small = [pltpu.make_async_copy(a, b, psem.at[i]) for i, (a, b) in enumerate(
        ((sf_hbm, sf_ref), (lf_hbm, lf_ref), (skip_hbm, skip_ref)))]
    for c in small:
        c.start()
    for c in local_k[2:] + local_q[2:]:
        c.start()

    local_x.wait()
    wing = rim_out.shape[1]
    for j in range(3):
        for g in range(2):
            rim_out[8 * g + 2 * j:8 * g + 2 * j + 2, :] = xb[j, rows - 2:rows, g * wing:(g + 1) * wing]

    @pl.when(z == 0)
    def _():
        gprev[...] = jnp.zeros_like(gprev)

    pl.semaphore_wait(barrier, count)
    if relayed:
        inner = (z > 0) & (z < n - 1)
        for step in (-1, 1):
            @pl.when(inner)
            def _():
                pl.semaphore_signal(
                    ready, inc=1, device_id={"ctx": jnp.clip(z + step, 0, n - 1)}, device_id_type=MESH)

    up = jnp.minimum(z + 1, n - 1)
    rim = remote(rim_out, rim_in, rim_s, rim_r, "ctx", up)

    def gate(h):
        return remote(gown.at[h], gprev.at[h], gate_s.at[h], gate_r.at[h], "ctx", up)

    @pl.when(z < n - 1)
    def _():
        rim.start()

    def each_query(h, act, least=1, most=None):
        for other in range(pivot, n - 1):
            @pl.when((other + least <= z) & (z <= other + (most or n)))
            def _():
                act(remote(
                    qbuf.at[h, pl.ds(0, rows)],
                    qbuf.at[h, pl.ds(pl.multiple_of((z - other) * rows, rows), rows)],
                    q_s.at[other - pivot, h], q_r.at[z - other, h], "ctx", other))

    def each_key(h, act):
        for other in range(1, pivot + 1):
            @pl.when((other > z) & (z < pivot))
            def _():
                act(remote(kbuf.at[own, h], kbuf.at[own, h], k_s.at[other, h], k_r.at[own, h], "ctx", other))

    def each_value(h, act):
        for other in range(1, pivot + 1):
            @pl.when((other > z) & (z < pivot))
            def _():
                act(remote(vbuf.at[own, h], vbuf.at[own, h], v_s.at[other, h], v_r.at[own, h], "ctx", other))

    early = min(2, heads)
    steady = max(early, heads - 2)
    for h in range(early):
        local_k[h].wait()
        local_q[h].wait()
        each_key(h, lambda c: c.start())
        each_query(h, lambda c: c.start(), 1, 1)

    for c in small:
        c.wait()

    def featured(h, size, edge):
        part = pl.ds(pl.multiple_of(h * HD, HD), HD)
        row = lax.broadcasted_iota(jnp.int32, (size, HD), 0)
        feats = []
        for j in range(3):
            x = xb[j, 0:size, part].astype(F32)
            last = edge[2 * j + 1:2 * j + 2] if edge is not None else 0.0
            prior = edge[2 * j:2 * j + 1] if edge is not None else 0.0
            x1 = jnp.where(row == 0, last, pltpu.roll(x, 1, 0))
            x2 = jnp.where(row == 0, prior, jnp.where(row == 1, last, pltpu.roll(x, 2, 0)))
            total = sf_ref[0, j:j + 1, part].astype(F32) * x
            total = total + sf_ref[1, j:j + 1, part].astype(F32) * x1
            feats.append(total + sf_ref[2, j:j + 1, part].astype(F32) * x2)
        f0[h, 0:size] = feats[0]
        gown[h, 0:size] = (feats[1] * feats[2]).astype(BF)

    @pl.loop(0, heads)
    def _(h):
        featured(h, rows, None)

        @pl.when((z == 0) & (h < early))
        def _():
            gate(h).start()

    for c in local_k[early:] + local_q[early:]:
        c.wait()

    if relayed:
        pl.semaphore_wait(ready, (z > 1).astype(jnp.int32) + (z < n - 2).astype(jnp.int32))

    @pl.loop(0, heads)
    def _(h):
        each_query(h, lambda c: c.start(), 2)

        @pl.when(h >= early)
        def _():
            each_query(h, lambda c: c.start(), 1, 1)

    @pl.when(z > 0)
    def _():
        rim.wait_recv()

    @pl.loop(0, heads)
    def _(h):
        @pl.when(z > 0)
        def _():
            both = rim_in[:, pl.ds(pl.multiple_of(lax.rem(h * HD, wing), HD), HD)].astype(F32)
            featured(h, 16, jnp.where(h * HD < wing, both[0:8], both[8:16]))

        @pl.when((z > 0) & (z < n - 1) & ((z >= pivot) | (h < early)))
        def _():
            gate(h).start()

    half = heads // 2
    local_w, over_core = [], []
    for g in range(2):
        for d in range(chips):
            def columns(side):
                return w_hbm.at[pl.ds(g * half, half), :, pl.ds(pl.multiple_of(there(d, side) * cols, cols), cols)]

            def place(lo):
                return wv.at[pl.ds(g * half, half), pl.ds(lo, HD), pl.ds(d * cols, cols)]
            local_w.append(pltpu.make_async_copy(columns(core), place(0), wsem.at[g, d]))
            over_core.append(remote(columns(1 - core), place(HD), pw_s.at[g, d], pw_r.at[g, d], "mp", partner))

    slab = late // parts
    bit = HD // 2
    chunks = [(d, side, e, i) for d, side in beyond for e in range(slab) for i in range(2)]

    def late_part(src, owner, e, i):
        return wl.at[src, owner * slab + e, pl.ds(i * bit, bit)]

    def over_x(src, b, e, i):
        return remote(
            w_hbm.at[sure + part_at * slab + e, pl.ds(i * bit, bit), pl.ds(pl.multiple_of(b * cols, cols), cols)],
            late_part(src, part_at, e, i), wx_s.at[b, e, i], wx_r.at[src, e, i], "mp", b)

    def over_y(src, owner, e, i, d):
        ref = late_part(src, owner, e, i)
        return remote(ref, ref, wy_s.at[d, src, e, i], wy_r.at[owner, src, e, i],
                      "parts", lax.rem(part_at + d, parts))

    for d, side, e, i in chunks:
        over_x(me, at_side(d, side), e, i).start()

    def swap(d, side, e, i):
        src = at_side(d, side)
        over_x(src, src, e, i).wait_recv()
        for k in range(1, parts):
            over_y(src, part_at, e, i, k).start()

    flip = (lax.broadcasted_iota(jnp.int32, (tap_count, 2 * rows), 0)
            + lax.broadcasted_iota(jnp.int32, (tap_count, 2 * rows), 1)) == rows
    based = dot(lf_ref[...], flip.astype(BF))
    for g in range(groups):
        wide = jnp.broadcast_to(based[g:g + 1], (rows, 2 * rows))
        taps[g] = pltpu.roll(wide, 0, 1, stride=1, stride_axis=0).astype(BF)
    acc[...] = jnp.zeros_like(acc)

    lane = lax.broadcasted_iota(jnp.int32, (rows, HD), 1) // width

    def mix(h):
        @pl.when(z > 0)
        def _():
            gate(h).wait_recv()

        mine = gown[h]
        both = jnp.concatenate([gprev[h], mine], axis=0)
        filt = jnp.zeros((rows, HD), F32)
        for g in range(per_tile):
            filt = jnp.where(lane == g, dot(taps[h * per_tile + g], both), filt)
        part = pl.ds(pl.multiple_of(h * HD, HD), HD)
        val = f0[h] * (filt + skip_ref[:, part] * mine.astype(F32))
        vbuf[own, h] = val.T.astype(BF)

    def key_and_gate(h):
        each_key(h, lambda c: c.start())

        @pl.when(z < n - 1)
        def _():
            gate(h).start()

    @pl.when(z < pivot)
    def _():
        @pl.loop(0, heads)
        def _(h):
            @pl.when(h >= steady)
            def _():
                key_and_gate(h)

            mix(h)
            each_value(h, lambda c: c.start())

            @pl.when(h + early < steady)
            def _():
                key_and_gate(h + early)

    for a, b in zip(local_w, over_core):
        a.start()
        b.start()

    scale = HD ** -0.5
    krow = lax.broadcasted_iota(jnp.int32, (rows, span), 0)
    kcol = lax.broadcasted_iota(jnp.int32, (rows, span), 1)

    def each_part(h, act):
        for s in range(1, slots):
            @pl.when((z >= pivot) & (z + s < n))
            def _():
                act(s,
                    remote(sbuf.at[s - 1, h], pbuf.at[z - pivot, h],
                           o_s.at[s - 1, h], o_r.at[z - pivot, h], "ctx", z + s),
                    remote(sstat.at[s - 1, h], pstat.at[z - pivot, h],
                           t_s.at[s - 1, h], t_r.at[z - pivot, h], "ctx", z + s))

    def hand_over(h):
        def act(s, o, t):
            gi, at = (s * rows) // span, (s * rows) % span
            mm = mst[h, gi, :, at:at + rows]
            ll = lst[h, gi, :, at:at + rows]
            aa = ast[h, gi, :, at:at + rows]
            sbuf[s - 1, h] = (aa * (1.0 / ll[0:1])).astype(BF)
            sstat[s - 1, h] = mm[0:1] + jnp.log(ll[0:1])
            o.start()
            t.start()
        each_part(h, act)

    def queries_in(h):
        for s in range(1, slots):
            @pl.when((z >= pivot) & (z + s < n))
            def _():
                remote(qbuf.at[h, pl.ds(0, rows)], qbuf.at[h, pl.ds(s * rows, rows)],
                       q_s.at[0, h], q_r.at[s, h], "ctx", jnp.minimum(z + s, n - 1)).wait_recv()

    def own_keys(h):
        queries_in(h)
        for gi in range(query_groups):
            q = qbuf[h, gi * span:(gi + 1) * span]
            s = dot(kbuf[own, h], q, 1, 1) * scale
            s = jnp.where(krow <= kcol + gi * span, s, NEG)
            mx = jnp.max(s, axis=0, keepdims=True)
            p = jnp.exp(s - mx)
            mst[h, gi] = jnp.broadcast_to(mx, (8, span))
            lst[h, gi] = jnp.broadcast_to(jnp.sum(p, axis=0, keepdims=True), (8, span))
            ast[h, gi] = dot(vbuf[own, h], p.astype(BF))

    def key_in(j, h):
        return remote(kbuf.at[j, h], kbuf.at[j, h], k_s.at[0, 0], k_r.at[j, h], "ctx", j)

    def value_in(j, h):
        return remote(vbuf.at[j, h], vbuf.at[j, h], v_s.at[0, 0], v_r.at[j, h], "ctx", j)

    @pl.when(z > pivot)
    def _():
        @pl.loop(0, heads)
        def _(h):
            mix(h)
            own_keys(h)
            hand_over(h)

    def finished(h):
        att[h] = (ast[h, 0, :, 0:rows] * (1.0 / lst[h, 0, 0:1, 0:rows])).T.astype(BF)

    def front(h):
        s = dot(kbuf[0, h], qbuf[h, 0:rows], 1, 1) * scale
        s = jnp.where(krow[:, 0:rows] <= kcol[:, 0:rows], s, NEG)
        p = jnp.exp(s - jnp.max(s, axis=0, keepdims=True))
        o = dot(vbuf[0, h], p.astype(BF)) * (1.0 / jnp.sum(p, axis=0, keepdims=True))
        att[h] = o.T.astype(BF)

    def hub(h):
        key_in(0, h).wait_recv()
        queries_in(h)
        s = dot(jnp.concatenate([kbuf[0, h], kbuf[1, h]], axis=0), qbuf[h], 1, 1) * scale
        krow2 = lax.broadcasted_iota(jnp.int32, (2 * rows, span), 0) - rows
        kcol2 = lax.broadcasted_iota(jnp.int32, (2 * rows, span), 1)
        s = jnp.where(krow2 <= kcol2, s, NEG)
        mx = jnp.max(s, axis=0, keepdims=True)
        p = jnp.exp(s - mx)
        total = jnp.sum(p, axis=0, keepdims=True)
        p = p.astype(BF)
        inv = 1.0 / total
        lse = mx + jnp.log(total)
        mix(h)
        value_in(0, h).wait_recv()
        o = dot(jnp.concatenate([vbuf[0, h], vbuf[1, h]], axis=1), p) * inv

        def act(s, c, t):
            at = slice(s * rows, (s + 1) * rows)
            sbuf[s - 1, h] = o[:, at].astype(BF)
            sstat[s - 1, h] = lse[:, at]
            c.start()
            t.start()
        each_part(h, act)
        att[h] = o[:, 0:rows].T.astype(BF)

    def rear(h):
        @pl.loop(0, jnp.maximum(z - pivot, 0))
        def _(turn):
            j = z - pivot - 1 - turn
            remote(sbuf.at[0, 0], pbuf.at[j, h], o_s.at[0, 0], o_r.at[j, h], "ctx", j + pivot).wait_recv()
            remote(sstat.at[0, 0], pstat.at[j, h], t_s.at[0, 0], t_r.at[j, h], "ctx", j + pivot).wait_recv()
            old = mst[h, 0, :, 0:rows]
            lse = pstat[j, h]
            mx = jnp.maximum(old, lse)
            fade, gain = jnp.exp(old - mx), jnp.exp(lse - mx)
            mst[h, 0, :, 0:rows] = mx
            lst[h, 0, :, 0:rows] = lst[h, 0, :, 0:rows] * fade + gain
            ast[h, 0, :, 0:rows] = ast[h, 0, :, 0:rows] * fade[0:1] + pbuf[j, h].astype(F32) * gain[0:1]
        finished(h)

    def one_head(h):
        if joint:
            @pl.when(z < pivot)
            def _():
                front(h)

            @pl.when(z == pivot)
            def _():
                hub(h)
        else:
            @pl.when(z <= pivot)
            def _():
                @pl.when(z == pivot)
                def _():
                    mix(h)

                own_keys(h)

                @pl.loop(0, z)
                def _(j):
                    key_in(j, h).wait_recv()
                    value_in(j, h).wait_recv()
                    for gi in range(query_groups):
                        q = qbuf[h, gi * span:(gi + 1) * span]
                        s = dot(kbuf[j, h], q, 1, 1) * scale
                        old = mst[h, gi, 0:1]
                        mx = jnp.maximum(old, jnp.max(s, axis=0, keepdims=True))
                        p = jnp.exp(s - mx)
                        fade = jnp.exp(old - mx)
                        mst[h, gi] = jnp.broadcast_to(mx, (8, span))
                        lst[h, gi] = jnp.broadcast_to(
                            lst[h, gi, 0:1] * fade + jnp.sum(p, axis=0, keepdims=True), (8, span))
                        ast[h, gi] = ast[h, gi] * fade + dot(vbuf[j, h], p.astype(BF))

                @pl.when(z == pivot)
                def _():
                    hand_over(h)

                finished(h)

        @pl.when(z > pivot)
        def _():
            rear(h)

    def beside(h):
        return remote(att.at[h], pat.at[h], pat_s.at[h], pat_r.at[h], "mp", partner)

    def gathered(src, l, b):
        return remote(att.at[sure + l], atl.at[src, l], at_s.at[b, l], at_r.at[src, l], "mp", b)

    pieces = 4
    piece = cols // pieces

    def along(d, i):
        return remote(s2.at[d, i], r2.at[d, i], b_s.at[d, i], b_r.at[d, i], "mp", there(d, core))

    def weights_in(g):
        for d in range(chips):
            local_w[g * chips + d].wait()
            over_core[g * chips + d].wait_recv()

    def both_cores(h):
        beside(h).wait_recv()
        return jnp.concatenate([att[h], pat[h]], axis=1)

    def project(h, blocks):
        lhs = both_cores(h)
        for d in range(blocks):
            acc[d] += dot(lhs, wv[h, :, d * cols:(d + 1) * cols])

    @pl.loop(0, sure)
    def _(h):
        one_head(h)
        beside(h).start()

        @pl.when(h == 1)
        def _():
            weights_in(0)

        @pl.when(h == half)
        def _():
            weights_in(1)

        @pl.when(h > 0)
        def _():
            project(h - 1, chips)

        for k, chunk in enumerate(chunks):
            @pl.when(h == min(sure - 1, 1 + k * (sure - 1) // len(chunks)))
            def _():
                swap(*chunk)

    if half >= sure:
        weights_in(1)
    if sure < 2:
        weights_in(0)
    for d in range(chips):
        acc[d] += dot(att[sure - 1], wv[sure - 1, 0:HD, d * cols:(d + 1) * cols])
    beside(sure - 1).wait_recv()
    lhs = pat[sure - 1]
    for d in range(1, chips):
        for i in range(pieces):
            at = slice(i * piece, (i + 1) * piece)
            s2[d, i] = (acc[d, :, at] + dot(
                lhs, wv[sure - 1, HD:, d * cols + i * piece:d * cols + (i + 1) * piece])).astype(BF)
            along(d, i).start()
    acc[0] += dot(lhs, wv[sure - 1, HD:, 0:cols])

    @pl.loop(0, late)
    def _(l):
        one_head(sure + l)
        for d, side in beyond:
            gathered(me, l, at_side(d, side)).start()
        beside(sure + l).start()

        @pl.when(l > 0)
        def _():
            project(sure + l - 1, 1)

    if late:
        project(heads - 1, 1)
    for c in over_core:
        c.wait_send()
    for d, side, e, i in chunks:
        src = at_side(d, side)
        over_x(me, src, e, i).wait_send()
        for k in range(1, parts):
            over_y(src, part_at, e, i, k).wait_send()
    for l in range(late):
        for d, side in beyond:
            gathered(me, l, at_side(d, side)).wait_send()

    @pl.when(z < n - 1)
    def _():
        rim.wait_send()

    @pl.loop(0, heads)
    def _(h):
        def ended(s, o, t):
            o.wait_send()
            t.wait_send()
        beside(h).wait_send()

        @pl.when(z < n - 1)
        def _():
            gate(h).wait_send()

        each_query(h, lambda c: c.wait_send())
        each_key(h, lambda c: c.wait_send())
        each_value(h, lambda c: c.wait_send())
        each_part(h, ended)

    for d, side, e, i in chunks:
        for k in range(1, parts):
            owner = lax.rem(part_at + parts - k, parts)
            over_y(at_side(d, side), owner, e, i, k).wait_recv()
    if late:
        for d, side in beyond:
            src = at_side(d, side)
            for l in range(late):
                gathered(src, l, src).wait_recv()
    for i in range(pieces):
        at = slice(i * piece, (i + 1) * piece)
        total = acc[0, :, at]
        if late:
            for d, side in beyond:
                src = at_side(d, side)
                lhs = jnp.concatenate([atl[src, l] for l in range(late)], axis=1)
                total = total + dot(lhs, wl[src, :, :, at].reshape(late * HD, piece))
        for d in range(1, chips):
            along(d, i).wait_recv()
            total = total + r2[d, i].astype(F32)
        out_ref[:, at] = total.astype(BF)

    for i in range(pieces):
        for d in range(1, chips):
            along(d, i).wait_send()


def per_device(n, m, parts_n, inputs, short_filter, long_filter, skip_gain, queries, key_rows, out_weight):
    rows, _, channels = inputs.shape
    heads = channels // HD
    groups = long_filter.shape[0]
    total = out_weight.shape[1]
    cols = total // m
    chips = m // 2
    pivot = n // 3
    slots = n - pivot
    batch = min(3, slots)
    padded = -(-slots // batch) * batch
    span = batch * rows
    gq = padded // batch
    parts = max(slots - 1, 1)
    late = LATE if LATE % parts_n == 0 and heads > LATE + 1 else 0
    slab = max(late // parts_n, 1)
    vm = pltpu.VMEM
    dma = pltpu.SemaphoreType.DMA
    scratch = [
        vm(short_filter.shape, BF), vm(long_filter.shape, BF), vm((1, channels), F32), dma((3,)),
        vm((3, rows, channels), BF), vm((16, channels // 2), BF), vm((16, channels // 2), BF),
        vm((heads, rows, HD), F32), vm((heads, rows, HD), BF), vm((heads, rows, HD), BF),
        vm((groups, rows, 2 * rows), BF),
        vm((pivot + 1, heads, rows, HD), BF), vm((pivot + 1, heads, HD, rows), BF),
        vm((heads, padded * rows, HD), BF),
        vm((heads, gq, 8, span), F32), vm((heads, gq, 8, span), F32), vm((heads, gq, HD, span), F32),
        vm((parts, heads, HD, rows), BF), vm((parts, heads, 1, rows), F32),
        vm((parts, heads, HD, rows), BF), vm((parts, heads, 1, rows), F32),
        vm((heads, rows, HD), BF), vm((heads, rows, HD), BF),
        vm((heads, 2 * HD, chips * cols), BF), vm((chips, rows, cols), F32),
        vm((chips, 4, rows, cols // 4), BF), vm((chips, 4, rows, cols // 4), BF),
        vm((m, max(late, 1), HD, cols), BF), vm((m, max(late, 1), rows, HD), BF),
        dma, dma((heads,)), dma((heads,)), dma((2, chips)), dma, dma, dma((heads,)), dma((heads,)),
    ] + [dma((pivot + 1, heads))] * 4 + [dma((slots, heads))] * 2 + [
        dma((parts, heads)), dma((parts, heads)), dma((parts, heads)), dma((parts, heads)),
    ] + [dma((chips, 4))] * 2 + [pltpu.SemaphoreType.REGULAR] + [
        dma((2, chips)), dma((2, chips)), dma((heads,)), dma((heads,)),
        dma((m, slab, 2)), dma((m, slab, 2)), dma((parts_n, m, slab, 2)), dma((parts_n, m, slab, 2)),
        dma((m, max(late, 1))), dma((m, max(late, 1))),
    ]
    in_vmem = pl.BlockSpec(memory_space=pltpu.VMEM)
    in_hbm = pl.BlockSpec(memory_space=pl.ANY)
    return pl.pallas_call(
        functools.partial(kernel, n, m, parts_n, late),
        out_shape=pltpu.VMEM((rows, cols), BF),
        in_specs=[in_hbm] * 7,
        out_specs=in_vmem,
        scratch_shapes=scratch,
        compiler_params=pltpu.CompilerParams(
            collective_id=0, has_side_effects=True, vmem_limit_bytes=60 * 2**20),
    )(inputs.transpose(1, 0, 2), short_filter, long_filter, skip_gain[None], queries, key_rows,
      out_weight.reshape(heads, HD, total))


def solution(mesh):
    placed = (
        P(("parts", "ctx"), None, "mp"),
        P(None, None, "mp"),
        P("mp", None),
        P("mp"),
        P(("parts", "ctx"), "mp"),
        P(("parts", "ctx"), "mp"),
        P("mp", None),
    )
    return jax.shard_map(
        functools.partial(per_device, mesh.shape["ctx"], mesh.shape["mp"], mesh.shape["parts"]),
        mesh=mesh, in_specs=placed, out_specs=P(("parts", "ctx"), "mp"), check_vma=False)
```
